32 devices in a mesh: tm: 8 (over z, x), frame: 4 (over y, core).
Axes of the slice: x: 2, y: 2, z: 4, core: 2. Of those that a mesh axis runs over, the one named last changes fastest.
Arguments:
- start_state: float32 [4, 32, 32, 128], P('frame'), may hold values from -6 to 6
- initial_guess: float32 [8, 4, 32, 32, 128], P('tm', 'frame'), may hold values from -6 to 6
- noise_draws: float32 [8, 4, 32, 32, 128], P('tm', 'frame'), may hold values from -6 to 6
- timesteps: int32 [8], P('tm'), may hold values from 0 to 999
- gain_space: float32 [128], replicated, may hold values from 0.1 to 1.9
- gain_attention: float32 [128], replicated, may hold values from 0.1 to 1.9
- time_weight: float32 [128, 256], replicated, may hold values from -0.5 to 0.5
- space_weight: bfloat16 [1152, 128], replicated, may hold values from -0.1875 to 0.1875
- attention_weight: bfloat16 [128, 384], replicated, may hold values from -4 to 4
- output_weight: bfloat16 [128, 128], replicated, may hold values from -0.5 to 0.5
Outputs:
- advanced: float32 [8, 4, 32, 32, 128], P('tm', 'frame')
The draws below stay inside these ranges and needn't reach their ends.
All inputs are finite; a program needn't handle non-finite values.
Results may differ from the reference program's by a relative error of at most 0.0025.
Values may be sent and summed in bfloat16 or wider, within the bound.
A program may use at most 64 MiB of HBM per device.

```python
import math
import jax
import jax.numpy as jnp
from jax import lax

C = 128
HEAD_DIM = 64
H = 32
W = 32
ITERS = 2
FRAMES = 4
STEPS = 8


def draw_attention_weight(key, part):
    drawn = jax.random.normal(jax.random.fold_in(key, 7), (C, 3 * C), jnp.float32) / math.sqrt(C)
    return jnp.clip(drawn, -4.0, 4.0).astype(jnp.bfloat16)


def touch_ends(values, stream_key, least, high):
    extent = values.shape
    index_at = [jax.random.randint(jax.random.fold_in(stream_key, axis), (), 0, extent[axis]) for axis in range(len(extent))]
    values = values.at[tuple(index_at)].set(least)
    longest = extent.index(max(extent))
    index_at[longest] = (index_at[longest] + 1) % extent[longest]
    return values.at[tuple(index_at)].set(high)


def shard_levels(own_key, extent, split, smallest, top_value):
    def one(position, parts):
        heights = jax.random.uniform(jax.random.fold_in(jax.random.fold_in(own_key, 6), position), (parts,), jnp.float32, smallest / len(split), top_value / len(split))
        return jnp.repeat(jnp.exp(heights), extent[position] // parts).reshape((-1,) + (1,) * (len(extent) - position - 1))

    level = one(*split[0])
    for cut in split[1:]:
        level = level * one(*cut)
    return level


def noise(key, extent, width, reach, pieces=(), kind=jnp.bfloat16):
    array = width * jax.random.normal(key, extent, jnp.float32)
    if pieces:
        array = array * shard_levels(key, extent, pieces, -0.22, 0.18)
    return jnp.clip(array, -reach, reach).astype(kind)


def setup_inputs(seed: int = 0) -> dict:
    keys = jax.random.split(jax.random.key(seed), 11)
    start_state = noise(keys[0], (FRAMES, H, W, C), 1.0, 6.0, ((0, 4),), jnp.float32)
    initial_guess = noise(keys[1], (STEPS, FRAMES, H, W, C), 1.0, 6.0, ((0, 8), (1, 4)), jnp.float32)
    noise_draws = noise(keys[2], (STEPS, FRAMES, H, W, C), 1.0, 6.0, ((0, 8), (1, 4)), jnp.float32)
    timesteps = touch_ends(jax.random.randint(keys[3], (STEPS,), 0, 1000), jax.random.fold_in(keys[3], 1), 0, 999).astype(jnp.int32)
    gain_space = jnp.clip(1.0 + 0.18 * jax.random.normal(keys[4], (C,), jnp.float32), 0.1, 1.9)
    gain_attention = jnp.clip(1.0 + 0.18 * jax.random.normal(keys[5], (C,), jnp.float32), 0.1, 1.9)
    time_weight = noise(keys[6], (C, 2 * C), C ** -0.5, 0.5, (), jnp.float32)
    space_weight = noise(keys[7], (9 * C, C), (9 * C) ** -0.5, 0.1875)
    attention_weight = draw_attention_weight(jax.random.fold_in(keys[10], 71), 0)
    output_weight = noise(keys[9], (C, C), C ** -0.5, 0.5)
    return {"start_state": start_state, "initial_guess": initial_guess, "noise_draws": noise_draws, "timesteps": timesteps, "gain_space": gain_space, "gain_attention": gain_attention, "time_weight": time_weight, "space_weight": space_weight, "attention_weight": attention_weight, "output_weight": output_weight}


def embed_time(step_value):
    half_width = C // 2
    frequency = jnp.exp(-math.log(10000.0) * jnp.arange(half_width, dtype=jnp.float32) / half_width)
    angles = step_value.astype(jnp.float32) * frequency
    return jnp.concatenate([jnp.cos(angles), jnp.sin(angles)])

def modulation(step_value, time_weight):
    encoded = embed_time(step_value)[None, :]
    shifted = jnp.dot(encoded, time_weight, precision=lax.Precision.HIGHEST, preferred_element_type=jnp.float32)[0]
    return (1.0 + shifted[:C], shifted[C:])

def normalize(field, gain):
    return field * lax.rsqrt(lax.optimization_barrier(jnp.mean(field * field, axis=-1, keepdims=True)) + 1e-06) * gain

def conv_taps(padded, space_weight):
    frames_here = padded.shape[0]
    rows_here = padded.shape[1] - 2
    cols_here = padded.shape[2] - 2
    shifted = [padded[:, row_shift:row_shift + rows_here, col_shift:col_shift + cols_here, :] for row_shift in range(3) for col_shift in range(3)]
    stacked = jnp.concatenate(shifted, axis=-1).reshape(-1, 9 * padded.shape[3])
    result = jnp.dot(stacked, space_weight, preferred_element_type=jnp.float32)
    return result.reshape(frames_here, rows_here, cols_here, space_weight.shape[1])

def attend(normed_in, attention_weight):
    frames_all, rows_here, cols_here, channels = normed_in.shape
    projected = jnp.dot(normed_in.reshape(-1, channels), attention_weight, preferred_element_type=jnp.float32).astype(jnp.bfloat16)
    projected = lax.optimization_barrier(projected).astype(jnp.float32)
    projected = projected.reshape(frames_all, rows_here, cols_here, 3, channels // HEAD_DIM, HEAD_DIM)
    query_vectors = projected[:, :, :, 0]
    key_vectors = projected[:, :, :, 1]
    value_vectors = projected[:, :, :, 2]
    scores = jnp.einsum('fxyhd,gxyhd->xyhfg', query_vectors, key_vectors) / math.sqrt(HEAD_DIM)
    weights = jax.nn.softmax(scores, axis=-1).astype(jnp.bfloat16)
    weights = lax.optimization_barrier(weights).astype(jnp.float32)
    attended = jnp.einsum('xyhfg,gxyhd->fxyhd', weights, value_vectors)
    return attended.reshape(frames_all, rows_here, cols_here, channels).astype(jnp.bfloat16)

def drift(state, step_value, gain_space, gain_attention, time_weight, space_weight, attention_weight, output_weight):
    scaling, offset = modulation(step_value, time_weight)
    normed = (normalize(state, gain_space) * scaling + offset).astype(jnp.bfloat16)
    padded = jnp.pad(normed, ((0, 0), (1, 1), (1, 1), (0, 0)))
    mixed_state = state + jax.nn.silu(conv_taps(padded, space_weight))
    attn_in = normalize(mixed_state, gain_attention).astype(jnp.bfloat16)
    attended = attend(attn_in, attention_weight)
    projected = jnp.dot(attended.reshape(-1, attended.shape[-1]), output_weight, preferred_element_type=jnp.float32)
    return mixed_state + projected.reshape(mixed_state.shape)

def reference(start_state, initial_guess, noise_draws, timesteps, gain_space, gain_attention, time_weight, space_weight, attention_weight, output_weight):
    steps_total = timesteps.shape[0]
    time_values = timesteps.astype(jnp.float32) / 1000.0
    coefficient = (0.5 + time_values) / math.sqrt(steps_total)

    def one_term(carried):
        state, noise_block, step_value, time_value, coeff_value = carried
        evaluated = drift(state, step_value, gain_space, gain_attention, time_weight, space_weight, attention_weight, output_weight)
        return coeff_value * (evaluated + time_value * noise_block)
    iterate = initial_guess
    before = jnp.zeros_like(initial_guess)
    terms = jnp.zeros_like(initial_guess)
    for picard_turn in range(ITERS):
        terms = lax.map(one_term, (iterate, noise_draws, timesteps, time_values, coefficient))
        before = jnp.cumsum(terms, axis=0) - terms
        iterate = start_state[None] + before
    return start_state[None] + (before + terms)
```

```python
import functools
import math

import jax
import jax.numpy as jnp
import numpy as np
from jax import lax
from jax.experimental import pallas as pl
from jax.experimental.pallas import tpu as pltpu
from jax.sharding import PartitionSpec as P

HEAD_DIM = 64
ITERS = 2
GROUPS = 2
EPS = 1e-06


def kernel(
    n_tm,
    n_frame,
    width,
    groups,
    step_ref,
    start_hbm,
    guess_hbm,
    noise_hbm,
    freq_hbm,
    gain_space_hbm,
    gain_attention_hbm,
    wtime_hbm,
    wconv_hbm,
    wattn_hbm,
    wout_hbm,
    out_ref,
    start_ref,
    guess_ref,
    noise_ref,
    freq_ref,
    gain_space_ref,
    gain_attention_ref,
    wtime_ref,
    wconv_ref,
    wattn_ref,
    wout_ref,
    select,
    spread,
    gather,
    state,
    taps,
    base,
    term,
    proj,
    ain,
    rin,
    aout,
    rout,
    tsend,
    xin,
    zin,
    ein,
    zout,
    sout,
    load,
    in_send,
    in_recv,
    out_send,
    out_recv,
    x_send,
    x_recv,
    z_send,
    z_recv,
    c_send,
    c_recv,
    e_send,
    e_recv,
    s_send,
):
    cells, channels = start_hbm.shape
    share = cells // n_frame
    piece = share // groups
    half = piece // 2
    pieces = n_frame * groups
    chips = n_frame // 2
    heads = channels // HEAD_DIM
    lanes = channels // n_frame
    copies = lanes // heads
    f32, bf16 = jnp.float32, jnp.bfloat16
    me_tm = lax.axis_index("tm")
    me = lax.axis_index("frame")
    my_chip, my_core = me // 2, lax.rem(me, 2)
    link, side = me_tm // 2, lax.rem(me_tm, 2)
    links = n_tm // 2
    has_prev = link > 0
    has_next = link < links - 1
    first_link = link == 0
    second_link = link == 1
    middle = jnp.logical_and(has_prev, jnp.logical_or(has_next, second_link))
    not_middle = jnp.logical_not(middle)
    other_side = me_tm + 1 - 2 * side
    own_half = pl.multiple_of(side * half, half)
    far_half = pl.multiple_of((1 - side) * half, half)
    own_rows, far_rows = pl.ds(own_half, half), pl.ds(far_half, half)

    last_slot = n_frame - 1
    far_slots = list(range(n_frame - 2))
    near_slots = [n_frame - 2, last_slot]
    others = list(range(last_slot))

    def peer(s):
        chip = lax.rem(my_chip + 1 + lax.div(s, 2), chips)
        return 2 * chip + lax.rem(my_core + s + lax.div(s + 2, n_frame), 2)

    def sender(s):
        chip = lax.rem(my_chip + 2 * chips - 1 - lax.div(s, 2), chips)
        return 2 * chip + lax.rem(my_core + s + lax.div(s + 2, n_frame), 2)

    def at_frame(f):
        return {"tm": me_tm, "frame": f}

    def at_tm(t):
        return {"tm": t, "frame": me}

    barrier = pltpu.get_barrier_semaphore()

    def greet(device):
        pl.semaphore_signal(barrier, inc=1, device_id=device, device_id_type=pl.DeviceIdType.MESH)

    for s in others:
        greet(at_frame(peer(s)))
    greet(at_tm(other_side))

    @pl.when(has_prev)
    def _():
        greet(at_tm(me_tm - 2))
        greet(at_tm(other_side - 2))

    def meet():
        pl.semaphore_wait(barrier, n_frame + 2 * has_next.astype(jnp.int32))

    pairs = [
        (freq_hbm, freq_ref),
        (gain_space_hbm, gain_space_ref),
        (wtime_hbm, wtime_ref),
        (guess_hbm, guess_ref),
        (wconv_hbm, wconv_ref),
        (gain_attention_hbm, gain_attention_ref),
        (noise_hbm, noise_ref),
        (wattn_hbm, wattn_ref),
        (wout_hbm, wout_ref),
        (start_hbm, start_ref),
    ]
    loads = [pltpu.make_async_copy(src, dst, load.at[i]) for i, (src, dst) in enumerate(pairs)]
    for copy in loads:
        copy.start()

    edge = jnp.zeros((width, 3 * channels), bf16)
    taps[0:width, :] = edge
    taps[cells + width : cells + 2 * width, :] = edge

    @pl.when(first_link)
    def _():
        zin[...] = jnp.zeros_like(zin)

    @pl.when(jnp.logical_not(second_link))
    def _():
        ein[...] = jnp.zeros_like(ein)

    row = lax.broadcasted_iota(jnp.int32, (n_frame * channels, channels), 0)
    lane = lax.broadcasted_iota(jnp.int32, (n_frame * channels, channels), 1)
    wanted = row // channels * lanes + row % channels // HEAD_DIM * copies
    select[...] = jnp.where(lane // copies * copies == wanted, 1.0 / math.sqrt(HEAD_DIM), 0.0).astype(bf16)
    gather[...] = jnp.where(row % channels == lane, 1.0, 0.0).astype(bf16)
    row = lax.broadcasted_iota(jnp.int32, (channels, n_frame * channels), 0)
    lane = lax.broadcasted_iota(jnp.int32, (channels, n_frame * channels), 1)
    wanted = lane // channels * lanes + lane % channels // HEAD_DIM * copies
    spread[...] = jnp.where(row == wanted, 1.0, 0.0).astype(bf16)

    for copy in loads[:3]:
        copy.wait()
    step = jnp.full((8, channels), step_ref[0].astype(f32))
    time_value = step[0:1, :] / 1000.0
    coefficient = (0.5 + time_value) / math.sqrt(n_tm)
    angles = step * freq_ref[...]
    position = lax.broadcasted_iota(jnp.int32, (8, channels), 1)
    encoded = jnp.where(position < channels // 2, jnp.cos(angles), jnp.sin(angles))
    shifted = jnp.dot(encoded, wtime_ref[...], precision=lax.Precision.HIGHEST, preferred_element_type=f32)
    gain_space = gain_space_ref[...] * (1.0 + shifted[0:1, :channels])
    offset = shifted[0:1, channels:]

    def inverse_rms(v):
        return lax.rsqrt(jnp.mean(v * v, axis=-1, keepdims=True) + EPS)

    column = lax.broadcasted_iota(jnp.int32, (piece, channels), 0) % width

    def make_taps(at, x):
        normed = x * inverse_rms(x) * gain_space + offset
        left = jnp.where(column == 0, 0.0, pltpu.roll(normed, 1, 0))
        right = jnp.where(column == width - 1, 0.0, pltpu.roll(normed, piece - 1, 0))
        to = pl.multiple_of(at + width, width)
        taps[pl.ds(to, piece), 0:channels] = left.astype(bf16)
        taps[pl.ds(to, piece), channels : 2 * channels] = normed.astype(bf16)
        taps[pl.ds(to, piece), 2 * channels : 3 * channels] = right.astype(bf16)

    def first_taps(i, _):
        at = pl.multiple_of(i * piece, piece)
        make_taps(at, guess_ref[pl.ds(at, piece), :])
        return 0

    loads[3].wait()
    lax.fori_loop(0, pieces, first_taps, 0)
    for copy in loads[4:7]:
        copy.wait()
    gain_attention = gain_attention_ref[...]

    def remote(src, dst, send, recv, device):
        return pltpu.make_async_remote_copy(
            src_ref=src,
            dst_ref=dst,
            send_sem=send,
            recv_sem=recv,
            device_id=device,
            device_id_type=pl.DeviceIdType.MESH,
        )

    for turn in range(ITERS):
        source = guess_ref if turn == 0 else state
        last = turn == ITERS - 1

        def in_copy(s, g):
            return remote(
                ain.at[turn, g, s], rin.at[turn, g, s], in_send.at[turn, g, s], in_recv.at[turn, g, s], at_frame(peer(s))
            )

        def out_copy(s, g):
            return remote(
                aout.at[turn, g, s],
                rout.at[turn, g, s],
                out_send.at[turn, g, s],
                out_recv.at[turn, g, s],
                at_frame(sender(s)),
            )

        def x_copy(i, rows):
            return remote(
                tsend.at[turn, i, rows],
                xin.at[turn, i, rows],
                x_send.at[turn, i],
                x_recv.at[turn, i],
                at_tm(other_side),
            )

        whole, first_half = pl.ds(0, piece), pl.ds(0, half)

        def chain_copy(i, src):
            return remote(
                src, zin.at[turn, i, own_rows], z_send.at[turn, i], z_recv.at[turn, i], at_tm(me_tm + 2)
            )

        def cross_copy(i):
            return remote(
                zout.at[turn, i],
                zin.at[turn, i, own_rows],
                c_send.at[turn, i],
                c_recv.at[turn, i],
                at_tm(other_side + 2),
            )

        def level_copy(i):
            return remote(
                sout.at[turn, i],
                zin.at[turn, i, own_rows],
                s_send.at[turn, i],
                c_recv.at[turn, i],
                at_tm(other_side),
            )

        def entry_copy(i):
            return remote(
                tsend.at[turn, i, far_rows],
                ein.at[turn, i],
                e_send.at[turn, i],
                e_recv.at[turn, i],
                at_tm(other_side + 2),
            )

        def rows_of(q, g):
            return pl.multiple_of(q * share + g * piece, piece)

        def mix(g, slots):
            at = [rows_of(peer(s), g) for s in slots]
            near = [
                jnp.concatenate([taps[pl.ds(a + r * width, piece), :] for r in range(3)], axis=1) for a in at
            ]
            total = jnp.dot(jnp.concatenate(near, axis=0), wconv_ref[...], preferred_element_type=f32)
            here = jnp.concatenate([source[pl.ds(a, piece), :] for a in at], axis=0)
            value = here + total * (0.5 + 0.5 * jnp.tanh(0.5 * total))
            normed = (value * inverse_rms(value) * gain_attention).astype(bf16)
            for k, s in enumerate(slots):
                rows = slice(k * piece, (k + 1) * piece)
                ain[turn, g, s] = normed[rows]
            for s in slots:
                if s != last_slot:
                    in_copy(s, g).start()
            for k, s in enumerate(slots):
                rows = slice(k * piece, (k + 1) * piece)
                base[g, s] = coefficient * (value[rows] + time_value * noise_ref[pl.ds(at[k], piece), :])

        def project(g, blocks, slots):
            result = jnp.dot(jnp.concatenate(blocks, axis=0), wattn_ref[...], preferred_element_type=f32).astype(bf16)
            for k, s in enumerate(slots):
                proj[g, s] = result[k * piece : (k + 1) * piece]

        def attend(g, slots):
            keys = [proj[g, k, :, channels : 2 * channels] for k in range(n_frame)]
            values = [proj[g, k, :, 2 * channels : 3 * channels] for k in range(n_frame)]
            products = jnp.concatenate(
                [
                    jnp.concatenate([proj[g, s, :, 0:channels] * key for key in keys], axis=1)
                    for s in slots
                ],
                axis=0,
            )
            scores = jnp.dot(products, select[...], preferred_element_type=f32)
            most = scores
            shift = lanes
            while shift < channels:
                most = jnp.maximum(most, pltpu.roll(most, shift, 1))
                shift *= 2
            raised = jnp.exp(scores - most)
            total = raised
            shift = lanes
            while shift < channels:
                total = total + pltpu.roll(total, shift, 1)
                shift *= 2
            weights = (raised * (1.0 / total)).astype(bf16)
            wide = jnp.dot(weights, spread[...], preferred_element_type=f32).astype(bf16)
            value = jnp.concatenate(values, axis=1)
            weighted = jnp.concatenate(
                [wide[k * piece : (k + 1) * piece] * value for k in range(len(slots))], axis=0
            )
            result = jnp.dot(weighted, gather[...], preferred_element_type=f32).astype(bf16)
            for k, s in enumerate(slots):
                aout[turn, g, s] = result[k * piece : (k + 1) * piece]
            for s in slots:
                if s != last_slot:
                    out_copy(s, g).start()

        def close(g, blocks, slots):
            result = jnp.dot(jnp.concatenate(blocks, axis=0), wout_ref[...], preferred_element_type=f32)
            for k, s in enumerate(slots):
                value = base[g, s] + coefficient * result[k * piece : (k + 1) * piece]
                term[g * n_frame + s] = value
                tsend[turn, g * n_frame + s] = value.astype(bf16)

            @pl.when(jnp.logical_and(first_link, has_next))
            def _():
                for s in slots:
                    i = g * n_frame + s
                    chain_copy(i, tsend.at[turn, i, own_rows]).start()
                    entry_copy(i).start()

            @pl.when(side == 0)
            def _():
                for s in slots:
                    x_copy(g * n_frame + s, whole).start()

            @pl.when(jnp.logical_and(side == 1, middle))
            def _():
                for s in slots:
                    x_copy(g * n_frame + s, first_half).start()

        def wait_x(i):
            @pl.when(side == 0)
            def _():
                x_copy(i, first_half).wait_recv()

            @pl.when(side == 1)
            def _():
                x_copy(i, whole).wait_recv()

        for g in range(groups):
            if turn == 0 and g == 0:
                meet()
            mix(g, far_slots)
        for g in range(groups):
            mix(g, near_slots)
        if turn == 0:
            for copy in loads[7:]:
                copy.wait()
        for g in range(groups):
            project(g, [ain[turn, g, last_slot]], [last_slot])
        for g in range(groups):
            for s in reversed(others):
                in_copy(s, g).wait_recv()
            project(g, [rin[turn, g, s] for s in others], others)
            attend(g, far_slots)
            attend(g, near_slots)
        for g in range(groups):
            close(g, [aout[turn, g, last_slot]], [last_slot])
        for g in range(groups):
            for s in reversed(others):
                out_copy(s, g).wait_recv()
            close(g, [rout[turn, g, s] for s in others], others)

        def earlier_own(i):
            return zin[turn, i, own_rows, :].astype(f32) + ein[turn, i].astype(f32)

        def chain(i, _):
            chain_copy(i, zout.at[turn, i]).wait_recv()

            @pl.when(second_link)
            def _():
                entry_copy(i).wait_recv()
                sout[turn, i] = earlier_own(i).astype(bf16)
                level_copy(i).start()

            wait_x(i)

            @pl.when(has_next)
            def _():
                mine = term[i, own_rows, :] + xin[turn, i, own_rows, :].astype(f32)
                zout[turn, i] = (earlier_own(i) + mine).astype(bf16)
                chain_copy(i, zout.at[turn, i]).start()
                cross_copy(i).start()

            return 0

        @pl.when(middle)
        def _():
            lax.fori_loop(0, pieces, chain, 0)

        def finish(i, _):
            @pl.when(jnp.logical_and(not_middle, has_prev))
            def _():
                chain_copy(i, zout.at[turn, i]).wait_recv()

            @pl.when(jnp.logical_and(not_middle, side == 1))
            def _():
                x_copy(i, whole).wait_recv()

            @pl.when(has_prev)
            def _():
                cross_copy(i).wait_recv()

            at = rows_of(peer(lax.rem(i, n_frame)), lax.div(i, n_frame))
            target = out_ref if last else state

            def settle(half_rows, earlier):
                beside = jnp.where(side == 1, xin[turn, i, half_rows, :].astype(f32), 0.0)
                before = earlier + beside
                if last:
                    before = before + term[i, half_rows, :]
                rows = pl.ds(pl.multiple_of(at + half_rows.start, half), half)
                target[rows, :] = start_ref[rows, :] + before

            settle(own_rows, earlier_own(i))
            settle(far_rows, zin[turn, i, far_rows, :].astype(f32))
            if not last:
                make_taps(at, state[pl.ds(at, piece), :])
            return 0

        lax.fori_loop(0, pieces, finish, 0)

        def sent(i, _):
            @pl.when(side == 0)
            def _():
                x_copy(i, whole).wait_send()

            @pl.when(jnp.logical_and(side == 1, middle))
            def _():
                x_copy(i, first_half).wait_send()

            @pl.when(has_next)
            def _():
                chain_copy(i, zout.at[turn, i]).wait_send()

            @pl.when(jnp.logical_and(first_link, has_next))
            def _():
                entry_copy(i).wait_send()

            @pl.when(second_link)
            def _():
                level_copy(i).wait_send()

            @pl.when(jnp.logical_and(has_prev, has_next))
            def _():
                cross_copy(i).wait_send()

            return 0

        lax.fori_loop(0, pieces, sent, 0)

        for g in range(groups):
            for s in others:
                in_copy(s, g).wait_send()
                out_copy(s, g).wait_send()


def shards(
    n_tm,
    n_frame,
    start_state,
    initial_guess,
    noise_draws,
    timesteps,
    gain_space,
    gain_attention,
    time_weight,
    space_weight,
    attention_weight,
    output_weight,
):
    _, height, width, channels = start_state.shape
    cells = height * width
    share = cells // n_frame
    groups = GROUPS if share // width % GROUPS == 0 else 1
    piece = share // groups
    pieces = n_frame * groups
    half_width = channels // 2
    frequency = np.exp(-math.log(10000.0) * np.arange(half_width) / half_width).astype(np.float32)
    frequency = np.concatenate([frequency, frequency])[None]
    f32, bf16 = jnp.float32, jnp.bfloat16
    dma, vmem = pltpu.SemaphoreType.DMA, pltpu.VMEM
    field = vmem((cells, channels), f32)
    row = vmem((1, channels), f32)
    exchange = vmem((ITERS, groups, n_frame, piece, channels), bf16)
    along = vmem((ITERS, pieces, piece, channels), bf16)
    halves = vmem((ITERS, pieces, piece // 2, channels), bf16)
    anywhere = pl.BlockSpec(memory_space=pl.ANY)
    total = pl.pallas_call(
        functools.partial(kernel, n_tm, n_frame, width, groups),
        out_shape=pltpu.VMEM((cells, channels), f32),
        in_specs=[pl.BlockSpec(memory_space=pltpu.SMEM)] + [anywhere] * 10,
        out_specs=pl.BlockSpec(memory_space=pltpu.VMEM),
        scratch_shapes=[
            field,
            field,
            field,
            row,
            row,
            row,
            vmem(time_weight.shape, f32),
            vmem(space_weight.shape, bf16),
            vmem(attention_weight.shape, bf16),
            vmem(output_weight.shape, bf16),
            vmem((n_frame * channels, channels), bf16),
            vmem((channels, n_frame * channels), bf16),
            vmem((n_frame * channels, channels), bf16),
            field,
            vmem((cells + 2 * width, 3 * channels), bf16),
            vmem((groups, n_frame, piece, channels), f32),
            vmem((pieces, piece, channels), f32),
            vmem((groups, n_frame, piece, 3 * channels), bf16),
            exchange,
            exchange,
            exchange,
            exchange,
            along,
            along,
            along,
            halves,
            halves,
            halves,
            dma((10,)),
            *([dma((ITERS, groups, n_frame))] * 4),
            *([dma((ITERS, pieces))] * 9),
        ],
        compiler_params=pltpu.CompilerParams(collective_id=0, has_side_effects=True, vmem_limit_bytes=32 << 20),
    )(
        timesteps,
        start_state.reshape(cells, channels),
        initial_guess.reshape(cells, channels),
        noise_draws.reshape(cells, channels),
        jnp.asarray(frequency),
        gain_space[None],
        gain_attention[None],
        time_weight,
        space_weight,
        attention_weight,
        output_weight,
    )
    return total.reshape(1, 1, height, width, channels)


def solution(mesh):
    return jax.shard_map(
        functools.partial(shards, mesh.shape["tm"], mesh.shape["frame"]),
        mesh=mesh,
        in_specs=(
            P("frame", None, None, None),
            P("tm", "frame", None, None, None),
            P("tm", "frame", None, None, None),
            P("tm"),
            P(),
            P(),
            P(),
            P(),
            P(),
            P(),
        ),
        out_specs=P("tm", "frame", None, None, None),
        check_vma=False,
    )
```

```python
import functools
import math

import jax
import jax.numpy as jnp
import numpy as np
from jax import lax
from jax.experimental import pallas as pl
from jax.experimental.pallas import tpu as pltpu
from jax.sharding import PartitionSpec as P

HEAD_DIM = 64
ITERS = 2
GROUPS = 2
EPS = 1e-06


def kernel(
    n_tm,
    n_frame,
    width,
    step_ref,
    start_hbm,
    guess_hbm,
    noise_hbm,
    freq_hbm,
    gain_space_hbm,
    gain_attention_hbm,
    wtime_hbm,
    wconv_hbm,
    wattn_hbm,
    wout_hbm,
    out_ref,
    start_ref,
    guess_ref,
    noise_ref,
    freq_ref,
    gain_space_ref,
    gain_attention_ref,
    wtime_ref,
    wconv_ref,
    wattn_ref,
    wout_ref,
    select,
    spread,
    gather,
    params,
    noises,
    states,
    taps,
    taps_two,
    base,
    term,
    term_two,
    proj,
    ain,
    rin,
    aout,
    rout,
    tsend,
    xin,
    zin,
    zout,
    fsend,
    fin,
    load,
    in_send,
    in_recv,
    out_send,
    out_recv,
    x_send,
    x_recv,
    z_send,
    z_recv,
    f_send,
    f_recv,
    m_send,
    m_recv,
):
    cells, channels = start_hbm.shape
    part = cells // 2
    piece = part // n_frame
    part_rows = part // width
    chips = n_frame // 2
    heads = channels // HEAD_DIM
    lanes = channels // n_frame
    copies = lanes // heads
    f32, bf16 = jnp.float32, jnp.bfloat16
    me_tm = lax.axis_index("tm")
    me = lax.axis_index("frame")
    my_chip, my_core = me // 2, lax.rem(me, 2)
    link, side = me_tm // 2, lax.rem(me_tm, 2)
    links = n_tm // 2
    has_prev = link > 0
    has_next = link < links - 1
    partner = me_tm + 1 - 2 * side

    last_slot = n_frame - 1
    far_slots = list(range(n_frame - 2))
    near_slots = [n_frame - 2, last_slot]
    others = list(range(last_slot))

    def peer(s):
        chip = lax.rem(my_chip + 1 + lax.div(s, 2), chips)
        return 2 * chip + lax.rem(my_core + s + lax.div(s + 2, n_frame), 2)

    def sender(s):
        chip = lax.rem(my_chip + 2 * chips - 1 - lax.div(s, 2), chips)
        return 2 * chip + lax.rem(my_core + s + lax.div(s + 2, n_frame), 2)

    def at_frame(f):
        return {"tm": me_tm, "frame": f}

    def at_tm(t):
        return {"tm": t, "frame": me}

    def aligned(n, size):
        return pl.ds(pl.multiple_of(n, size), size)

    def in_part(s):
        return aligned(peer(s) * piece, piece)

    def in_frame(h, s):
        return aligned(h * part + peer(s) * piece, piece)

    own_start, far_start = side * part, (1 - side) * part
    edge_row = aligned((part_rows - 1 + side) * width, width)
    halo_row = aligned((part_rows - side) * width, width)
    halo = pl.ds(part, width)

    barrier = pltpu.get_barrier_semaphore()

    def greet(device):
        pl.semaphore_signal(barrier, inc=1, device_id=device, device_id_type=pl.DeviceIdType.MESH)

    for s in others:
        greet(at_frame(peer(s)))
    greet(at_tm(partner))

    @pl.when(has_prev)
    def _():
        greet(at_tm(me_tm - 2))

    def meet():
        pl.semaphore_wait(barrier, n_frame + has_next.astype(jnp.int32))

    pairs = [
        (freq_hbm, freq_ref),
        (gain_space_hbm, gain_space_ref),
        (wtime_hbm, wtime_ref),
        (guess_hbm, guess_ref),
        (wconv_hbm, wconv_ref),
        (gain_attention_hbm, gain_attention_ref),
        (noise_hbm, noise_ref),
        (wattn_hbm, wattn_ref),
        (wout_hbm, wout_ref),
        (start_hbm, start_ref),
        (noise_hbm.at[aligned(own_start, part)], noises.at[side]),
    ]
    loads = [pltpu.make_async_copy(src, dst, load.at[i]) for i, (src, dst) in enumerate(pairs)]
    for copy in loads:
        copy.start()

    edge = jnp.zeros((width, 3 * channels), bf16)
    taps[0:width, :] = edge
    taps[cells + width : cells + 2 * width, :] = edge
    for g in range(2):
        taps_two[g, aligned(side * (part + width), width), :] = edge

    @pl.when(jnp.logical_not(has_prev))
    def _():
        zin[...] = jnp.zeros_like(zin)

    row = lax.broadcasted_iota(jnp.int32, (n_frame * channels, channels), 0)
    lane = lax.broadcasted_iota(jnp.int32, (n_frame * channels, channels), 1)
    wanted = row // channels * lanes + row % channels // HEAD_DIM * copies
    select[...] = jnp.where(lane // copies * copies == wanted, 1.0 / math.sqrt(HEAD_DIM), 0.0).astype(bf16)
    gather[...] = jnp.where(row % channels == lane, 1.0, 0.0).astype(bf16)
    row = lax.broadcasted_iota(jnp.int32, (channels, n_frame * channels), 0)
    lane = lax.broadcasted_iota(jnp.int32, (channels, n_frame * channels), 1)
    wanted = lane // channels * lanes + lane % channels // HEAD_DIM * copies
    spread[...] = jnp.where(row == wanted, 1.0, 0.0).astype(bf16)

    for copy in loads[:3]:
        copy.wait()
    step = jnp.full((8, channels), step_ref[0].astype(f32))
    time_value = step[0:1, :] / 1000.0
    coefficient = (0.5 + time_value) / math.sqrt(n_tm)
    angles = step * freq_ref[...]
    position = lax.broadcasted_iota(jnp.int32, (8, channels), 1)
    encoded = jnp.where(position < channels // 2, jnp.cos(angles), jnp.sin(angles))
    shifted = jnp.dot(encoded, wtime_ref[...], precision=lax.Precision.HIGHEST, preferred_element_type=f32)
    gain_space = gain_space_ref[...] * (1.0 + shifted[0:1, :channels])
    offset = shifted[0:1, channels:]
    for k, value in enumerate((gain_space, offset, coefficient, time_value)):
        params[side, k : k + 1, :] = value

    def inverse_rms(v):
        return lax.rsqrt(jnp.mean(v * v, axis=-1, keepdims=True) + EPS)

    def make_taps(x, gain, shift, put):
        rows = x.shape[0]
        column = lax.broadcasted_iota(jnp.int32, x.shape, 0) % width
        normed = x * inverse_rms(x) * gain + shift
        left = jnp.where(column == 0, 0.0, pltpu.roll(normed, 1, 0))
        right = jnp.where(column == width - 1, 0.0, pltpu.roll(normed, rows - 1, 0))
        for k, value in enumerate((left, normed, right)):
            put(slice(k * channels, (k + 1) * channels), value.astype(bf16))

    def first_taps(i, _):
        at = i * piece

        def put(columns, value):
            taps[pl.ds(pl.multiple_of(at + width, width), piece), columns] = value

        make_taps(guess_ref[aligned(at, piece), :], gain_space, offset, put)
        return 0

    loads[3].wait()
    lax.fori_loop(0, 2 * n_frame, first_taps, 0)
    for copy in loads[4:7]:
        copy.wait()
    gain_attention = gain_attention_ref[...]

    def remote(src, dst, send, recv, device):
        return pltpu.make_async_remote_copy(
            src_ref=src,
            dst_ref=dst,
            send_sem=send,
            recv_sem=recv,
            device_id=device,
            device_id_type=pl.DeviceIdType.MESH,
        )

    def x_copy(s):
        return remote(
            tsend.at[in_frame(1 - side, s)], xin.at[in_part(s)], x_send.at[s], x_recv.at[s], at_tm(partner)
        )

    def x_halo():
        return remote(tsend.at[edge_row], xin.at[halo], x_send.at[n_frame], x_recv.at[n_frame], at_tm(partner))

    def noise_copy():
        return remote(
            noise_ref.at[aligned(far_start, part)], noises.at[side], m_send.at[0], m_recv.at[0], at_tm(partner)
        )

    def noise_arrival():
        return remote(
            noise_ref.at[aligned(far_start, part)], noises.at[1 - side], m_send.at[0], m_recv.at[0], at_tm(partner)
        )

    def params_copy(to):
        return remote(params.at[side], params.at[to], m_send.at[1], m_recv.at[1], at_tm(partner))

    def f_copy(s):
        return remote(fsend.at[in_part(s)], fin.at[in_part(s)], f_send.at[s], f_recv.at[s], at_tm(partner))

    def z_copy(turn, i, rows):
        return remote(
            zout.at[turn, rows], zin.at[turn, rows], z_send.at[turn, i], z_recv.at[turn, i], at_tm(me_tm + 2)
        )

    for turn in range(ITERS):
        last = turn == ITERS - 1

        def in_copy(s, g):
            return remote(
                ain.at[turn, g, s], rin.at[turn, g, s], in_send.at[turn, g, s], in_recv.at[turn, g, s], at_frame(peer(s))
            )

        def out_copy(s, g):
            return remote(
                aout.at[turn, g, s],
                rout.at[turn, g, s],
                out_send.at[turn, g, s],
                out_recv.at[turn, g, s],
                at_frame(sender(s)),
            )

        def group(g):
            return (1 - side if g == 0 else side) if turn == 0 else g

        def near_rows(g, s, r):
            if turn == 0:
                return taps[pl.ds(pl.multiple_of(group(g) * part + peer(s) * piece + r * width, width), piece), :]
            return taps_two[g, pl.ds(pl.multiple_of(peer(s) * piece + r * width, width), piece), :]

        def mix(g, slots):
            near = [jnp.concatenate([near_rows(g, s, r) for r in range(3)], axis=1) for s in slots]
            total = jnp.dot(jnp.concatenate(near, axis=0), wconv_ref[...], preferred_element_type=f32)
            if turn == 0:
                here = [guess_ref[in_frame(group(g), s), :] for s in slots]
                noise = [noise_ref[in_frame(group(g), s), :] for s in slots]
                scale, value_of_time = coefficient, time_value
            else:
                here = [states[g, in_part(s), :] for s in slots]
                noise = [noises[g, in_part(s), :] for s in slots]
                scale, value_of_time = params[g, 2:3, :], params[g, 3:4, :]
            value = jnp.concatenate(here, axis=0) + total * (0.5 + 0.5 * jnp.tanh(0.5 * total))
            normed = (value * inverse_rms(value) * gain_attention).astype(bf16)
            for k, s in enumerate(slots):
                ain[turn, g, s] = normed[k * piece : (k + 1) * piece]
            for s in slots:
                if s != last_slot:
                    in_copy(s, g).start()
            for k, s in enumerate(slots):
                base[g, s] = scale * (value[k * piece : (k + 1) * piece] + value_of_time * noise[k])

        def project(g, blocks, slots):
            result = jnp.dot(jnp.concatenate(blocks, axis=0), wattn_ref[...], preferred_element_type=f32).astype(bf16)
            for k, s in enumerate(slots):
                proj[g, s] = result[k * piece : (k + 1) * piece]

        def attend(g, slots):
            keys = [proj[g, k, :, channels : 2 * channels] for k in range(n_frame)]
            values = [proj[g, k, :, 2 * channels : 3 * channels] for k in range(n_frame)]
            products = jnp.concatenate(
                [
                    jnp.concatenate([proj[g, s, :, 0:channels] * key for key in keys], axis=1)
                    for s in slots
                ],
                axis=0,
            )
            scores = jnp.dot(products, select[...], preferred_element_type=f32)
            most = scores
            shift = lanes
            while shift < channels:
                most = jnp.maximum(most, pltpu.roll(most, shift, 1))
                shift *= 2
            raised = jnp.exp(scores - most)
            total = raised
            shift = lanes
            while shift < channels:
                total = total + pltpu.roll(total, shift, 1)
                shift *= 2
            weights = (raised * (1.0 / total)).astype(bf16)
            wide = jnp.dot(weights, spread[...], preferred_element_type=f32).astype(bf16)
            value = jnp.concatenate(values, axis=1)
            weighted = jnp.concatenate(
                [wide[k * piece : (k + 1) * piece] * value for k in range(len(slots))], axis=0
            )
            result = jnp.dot(weighted, gather[...], preferred_element_type=f32).astype(bf16)
            for k, s in enumerate(slots):
                aout[turn, g, s] = result[k * piece : (k + 1) * piece]
            for s in slots:
                if s != last_slot:
                    out_copy(s, g).start()

        def close(g, blocks, slots):
            result = jnp.dot(jnp.concatenate(blocks, axis=0), wout_ref[...], preferred_element_type=f32)
            scale = coefficient if turn == 0 else params[g, 2:3, :]
            for k, s in enumerate(slots):
                value = base[g, s] + scale * result[k * piece : (k + 1) * piece]
                if turn == 0:
                    term[in_frame(group(g), s), :] = value
                    tsend[in_frame(group(g), s), :] = value.astype(bf16)
                else:
                    term_two[g, s] = value
            if turn == 0 and g == 0:
                for s in slots:
                    x_copy(s).start()
            if last and g == GROUPS - 1:
                settle(slots)

        def settle(slots):
            for s in slots:
                @pl.when(has_prev)
                def _():
                    z_copy(turn, s, in_part(s)).wait_recv()

                first = zin[turn, in_part(s), :].astype(f32) + term_two[0, s]
                second = first + term_two[1, s]
                zout[turn, in_part(s), :] = second.astype(bf16)
                fsend[in_part(s), :] = jnp.where(side == 0, second, first).astype(bf16)
                f_copy(s).start()

                @pl.when(has_next)
                def _():
                    z_copy(turn, s, in_part(s)).start()

                mine = in_frame(side, s)
                out_ref[mine, :] = start_ref[mine, :] + jnp.where(side == 0, first, second)

        for g in range(GROUPS):
            if turn == 0 and g == 0:
                meet()
            mix(g, far_slots)
        for g in range(GROUPS):
            mix(g, near_slots)
        if turn == 0:
            params_copy(side).start()
            noise_copy().start()
            for copy in loads[7:]:
                copy.wait()
        for g in range(GROUPS):
            project(g, [ain[turn, g, last_slot]], [last_slot])
        for g in range(GROUPS):
            for s in reversed(others):
                in_copy(s, g).wait_recv()
            project(g, [rin[turn, g, s] for s in others], others)
            attend(g, far_slots)
            attend(g, near_slots)
        for g in range(GROUPS):
            close(g, [aout[turn, g, last_slot]], [last_slot])
            for s in others:
                in_copy(s, g).wait_send()
        for g in range(GROUPS):
            for s in reversed(others):
                out_copy(s, g).wait_recv()
            close(g, [rout[turn, g, s] for s in others], others)

        if not last:
            x_halo().start()

            def chain(i, rows, nat):
                z_copy_i = z_copy(turn, i, rows)

                @pl.when(has_prev)
                def _():
                    z_copy_i.wait_recv()

                total = zin[turn, rows, :].astype(f32) + (term[nat, :] + xin[rows, :].astype(f32))
                zout[turn, rows, :] = total.astype(bf16)
                z_copy_i.start()

            def chain_slot(s, _):
                x_copy(s).wait_recv()
                chain(s, in_part(s), in_frame(side, s))
                return 0

            @pl.when(has_next)
            def _():
                lax.fori_loop(0, n_frame, chain_slot, 0)
                x_halo().wait_recv()
                chain(n_frame, halo, halo_row)

            for g in range(GROUPS):
                for s in others:
                    out_copy(s, g).wait_send()
            params_copy(1 - side).wait_recv()
            noise_arrival().wait_recv()
            noise_copy().wait_send()
            params_copy(side).wait_send()

            def begin(i, rows, nat, arrival, at, keep):
                @pl.when(jnp.logical_not(has_next))
                def _():
                    arrival.wait_recv()

                    @pl.when(has_prev)
                    def _():
                        z_copy(turn, i, rows).wait_recv()

                first = start_ref[nat, :] + zin[turn, rows, :].astype(f32)
                second = first + jnp.where(side == 0, term[nat, :], xin[rows, :].astype(f32))
                for g, x in enumerate((first, second)):
                    if keep:
                        states[g, rows, :] = x

                    def put(columns, value):
                        taps_two[g, pl.ds(pl.multiple_of(at, width), x.shape[0]), columns] = value

                    make_taps(x, params[g, 0:1, :], params[g, 1:2, :], put)

            def begin_slot(s, _):
                begin(s, in_part(s), in_frame(side, s), x_copy(s), peer(s) * piece + width, True)
                return 0

            lax.fori_loop(0, n_frame, begin_slot, 0)
            begin(n_frame, halo, halo_row, x_halo(), (1 - side) * (part + width), False)

            def sent(s, _):
                x_copy(s).wait_send()

                @pl.when(has_next)
                def _():
                    z_copy(turn, s, in_part(s)).wait_send()

                return 0

            lax.fori_loop(0, n_frame, sent, 0)
            x_halo().wait_send()

            @pl.when(has_next)
            def _():
                z_copy(turn, n_frame, halo).wait_send()

    def receive(s, _):
        f_copy(s).wait_recv()
        rows = in_frame(1 - side, s)
        out_ref[rows, :] = start_ref[rows, :] + fin[in_part(s), :].astype(f32)
        return 0

    lax.fori_loop(0, n_frame, receive, 0)

    def sent_last(s, _):
        f_copy(s).wait_send()

        @pl.when(has_next)
        def _():
            z_copy(ITERS - 1, s, in_part(s)).wait_send()

        return 0

    lax.fori_loop(0, n_frame, sent_last, 0)
    for g in range(GROUPS):
        for s in others:
            remote(
                aout.at[ITERS - 1, g, s],
                rout.at[ITERS - 1, g, s],
                out_send.at[ITERS - 1, g, s],
                out_recv.at[ITERS - 1, g, s],
                at_frame(sender(s)),
            ).wait_send()


def shards(
    n_tm,
    n_frame,
    start_state,
    initial_guess,
    noise_draws,
    timesteps,
    gain_space,
    gain_attention,
    time_weight,
    space_weight,
    attention_weight,
    output_weight,
):
    _, height, width, channels = start_state.shape
    cells = height * width
    part = cells // 2
    piece = part // n_frame
    half_width = channels // 2
    frequency = np.exp(-math.log(10000.0) * np.arange(half_width) / half_width).astype(np.float32)
    frequency = np.concatenate([frequency, frequency])[None]
    f32, bf16 = jnp.float32, jnp.bfloat16
    dma, vmem = pltpu.SemaphoreType.DMA, pltpu.VMEM
    field = vmem((cells, channels), f32)
    row = vmem((1, channels), f32)
    exchange = vmem((ITERS, GROUPS, n_frame, piece, channels), bf16)
    carried = vmem((ITERS, part + width, channels), bf16)
    anywhere = pl.BlockSpec(memory_space=pl.ANY)
    total = pl.pallas_call(
        functools.partial(kernel, n_tm, n_frame, width),
        out_shape=pltpu.VMEM((cells, channels), f32),
        in_specs=[pl.BlockSpec(memory_space=pltpu.SMEM)] + [anywhere] * 10,
        out_specs=pl.BlockSpec(memory_space=pltpu.VMEM),
        scratch_shapes=[
            field,
            field,
            field,
            row,
            row,
            row,
            vmem(time_weight.shape, f32),
            vmem(space_weight.shape, bf16),
            vmem(attention_weight.shape, bf16),
            vmem(output_weight.shape, bf16),
            vmem((n_frame * channels, channels), bf16),
            vmem((channels, n_frame * channels), bf16),
            vmem((n_frame * channels, channels), bf16),
            vmem((2, 8, channels), f32),
            vmem((2, part, channels), f32),
            vmem((2, part, channels), f32),
            vmem((cells + 2 * width, 3 * channels), bf16),
            vmem((2, part + 2 * width, 3 * channels), bf16),
            vmem((GROUPS, n_frame, piece, channels), f32),
            field,
            vmem((GROUPS, n_frame, piece, channels), f32),
            vmem((GROUPS, n_frame, piece, 3 * channels), bf16),
            exchange,
            exchange,
            exchange,
            exchange,
            vmem((cells, channels), bf16),
            vmem((part + width, channels), bf16),
            carried,
            carried,
            vmem((part, channels), bf16),
            vmem((part, channels), bf16),
            dma((11,)),
            *([dma((ITERS, GROUPS, n_frame))] * 4),
            *([dma((n_frame + 1,))] * 2),
            *([dma((ITERS, n_frame + 1))] * 2),
            *([dma((n_frame,))] * 2),
            *([dma((2,))] * 2),
        ],
        compiler_params=pltpu.CompilerParams(collective_id=0, has_side_effects=True),
    )(
        timesteps,
        start_state.reshape(cells, channels),
        initial_guess.reshape(cells, channels),
        noise_draws.reshape(cells, channels),
        jnp.asarray(frequency),
        gain_space[None],
        gain_attention[None],
        time_weight,
        space_weight,
        attention_weight,
        output_weight,
    )
    return total.reshape(1, 1, height, width, channels)


def solution(mesh):
    return jax.shard_map(
        functools.partial(shards, mesh.shape["tm"], mesh.shape["frame"]),
        mesh=mesh,
        in_specs=(
            P("frame", None, None, None),
            P("tm", "frame", None, None, None),
            P("tm", "frame", None, None, None),
            P("tm"),
            P(),
            P(),
            P(),
            P(),
            P(),
            P(),
        ),
        out_specs=P("tm", "frame", None, None, None),
        check_vma=False,
    )
```

```python
import functools
import math

import jax
import jax.numpy as jnp
import numpy as np
from jax import lax
from jax.experimental import pallas as pl
from jax.experimental.pallas import tpu as pltpu
from jax.sharding import PartitionSpec as P

HEAD_DIM = 64
ITERS = 2
GROUPS = 2
EPS = 1e-06


def kernel(
    n_tm,
    n_frame,
    width,
    step_ref,
    start_hbm,
    guess_hbm,
    noise_hbm,
    freq_hbm,
    gain_space_hbm,
    gain_attention_hbm,
    wtime_hbm,
    wconv_hbm,
    wattn_hbm,
    wout_hbm,
    out_ref,
    start_ref,
    guess_ref,
    noise_ref,
    freq_ref,
    gain_space_ref,
    gain_attention_ref,
    wtime_ref,
    wconv_ref,
    wattn_ref,
    wout_ref,
    same_cell,
    params,
    noises,
    states,
    taps,
    taps_two,
    base,
    term,
    term_two,
    proj,
    ain,
    rin,
    aout,
    rout,
    tsend,
    xin,
    zin,
    zout,
    fsend,
    fin,
    load,
    in_send,
    in_recv,
    out_send,
    out_recv,
    x_send,
    x_recv,
    z_send,
    z_recv,
    f_send,
    f_recv,
    m_send,
    m_recv,
):
    cells, channels = start_hbm.shape
    part = cells // 2
    piece = part // n_frame
    part_rows = part // width
    chips = n_frame // 2
    heads = channels // HEAD_DIM
    block = min(max(16, 128 // n_frame), piece)
    f32, bf16 = jnp.float32, jnp.bfloat16
    me_tm = lax.axis_index("tm")
    me = lax.axis_index("frame")
    my_chip, my_core = me // 2, lax.rem(me, 2)
    link, side = me_tm // 2, lax.rem(me_tm, 2)
    links = n_tm // 2
    has_prev = link > 0
    has_next = link < links - 1
    partner = me_tm + 1 - 2 * side

    last_slot = n_frame - 1
    far_slots = list(range(n_frame - 2))
    near_slots = [n_frame - 2, last_slot]
    others = list(range(last_slot))

    def peer(s):
        chip = lax.rem(my_chip + 1 + lax.div(s, 2), chips)
        return 2 * chip + lax.rem(my_core + s + lax.div(s + 2, n_frame), 2)

    def sender(s):
        chip = lax.rem(my_chip + 2 * chips - 1 - lax.div(s, 2), chips)
        return 2 * chip + lax.rem(my_core + s + lax.div(s + 2, n_frame), 2)

    def at_frame(f):
        return {"tm": me_tm, "frame": f}

    def at_tm(t):
        return {"tm": t, "frame": me}

    def aligned(n, size):
        return pl.ds(pl.multiple_of(n, size), size)

    def in_part(s):
        return aligned(peer(s) * piece, piece)

    def in_frame(h, s):
        return aligned(h * part + peer(s) * piece, piece)

    own_start, far_start = side * part, (1 - side) * part
    edge_row = aligned((part_rows - 1 + side) * width, width)
    halo_row = aligned((part_rows - side) * width, width)
    halo = pl.ds(part, width)

    barrier = pltpu.get_barrier_semaphore()

    def greet(device):
        pl.semaphore_signal(barrier, inc=1, device_id=device, device_id_type=pl.DeviceIdType.MESH)

    for s in others:
        greet(at_frame(peer(s)))
    greet(at_tm(partner))

    @pl.when(has_prev)
    def _():
        greet(at_tm(me_tm - 2))

    def meet():
        pl.semaphore_wait(barrier, n_frame + has_next.astype(jnp.int32))

    pairs = [
        (freq_hbm, freq_ref),
        (gain_space_hbm, gain_space_ref),
        (wtime_hbm, wtime_ref),
        (guess_hbm, guess_ref),
        (wconv_hbm, wconv_ref),
        (gain_attention_hbm, gain_attention_ref),
        (noise_hbm, noise_ref),
        (wattn_hbm, wattn_ref),
        (wout_hbm, wout_ref),
        (start_hbm, start_ref),
        (noise_hbm.at[aligned(own_start, part)], noises.at[side]),
    ]
    loads = [pltpu.make_async_copy(src, dst, load.at[i]) for i, (src, dst) in enumerate(pairs)]
    for copy in loads:
        copy.start()

    edge = jnp.zeros((width, 3 * channels), bf16)
    taps[0:width, :] = edge
    taps[cells + width : cells + 2 * width, :] = edge
    for g in range(2):
        taps_two[g, aligned(side * (part + width), width), :] = edge

    @pl.when(jnp.logical_not(has_prev))
    def _():
        zin[...] = jnp.zeros_like(zin)

    row = lax.broadcasted_iota(jnp.int32, (n_frame * block, n_frame * block), 0)
    lane = lax.broadcasted_iota(jnp.int32, (n_frame * block, n_frame * block), 1)
    same_cell[...] = jnp.where(row % block == lane % block, 0.0, -jnp.inf)
    head_lane = lax.broadcasted_iota(jnp.int32, (n_frame * block, channels), 1) // HEAD_DIM
    heads_of = jnp.where(
        lax.broadcasted_iota(jnp.int32, (8, channels), 0) == lax.broadcasted_iota(jnp.int32, (8, channels), 1) // HEAD_DIM,
        1.0,
        0.0,
    ).astype(bf16)

    for copy in loads[:3]:
        copy.wait()
    step = jnp.full((8, channels), step_ref[0].astype(f32))
    time_value = step[0:1, :] / 1000.0
    coefficient = (0.5 + time_value) / math.sqrt(n_tm)
    angles = step * freq_ref[...]
    position = lax.broadcasted_iota(jnp.int32, (8, channels), 1)
    encoded = jnp.where(position < channels // 2, jnp.cos(angles), jnp.sin(angles))
    shifted = jnp.dot(encoded, wtime_ref[...], precision=lax.Precision.HIGHEST, preferred_element_type=f32)
    gain_space = gain_space_ref[...] * (1.0 + shifted[0:1, :channels])
    offset = shifted[0:1, channels:]
    for k, value in enumerate((gain_space, offset, coefficient, time_value)):
        params[side, k : k + 1, :] = value

    def inverse_rms(v):
        return lax.rsqrt(jnp.mean(v * v, axis=-1, keepdims=True) + EPS)

    def make_taps(x, gain, shift, put):
        rows = x.shape[0]
        column = lax.broadcasted_iota(jnp.int32, x.shape, 0) % width
        normed = x * inverse_rms(x) * gain + shift
        left = jnp.where(column == 0, 0.0, pltpu.roll(normed, 1, 0))
        right = jnp.where(column == width - 1, 0.0, pltpu.roll(normed, rows - 1, 0))
        for k, value in enumerate((left, normed, right)):
            put(slice(k * channels, (k + 1) * channels), value.astype(bf16))

    def first_taps(i, _):
        at = i * piece

        def put(columns, value):
            taps[pl.ds(pl.multiple_of(at + width, width), piece), columns] = value

        make_taps(guess_ref[aligned(at, piece), :], gain_space, offset, put)
        return 0

    loads[3].wait()
    lax.fori_loop(0, 2 * n_frame, first_taps, 0)
    for copy in loads[4:7]:
        copy.wait()
    gain_attention = gain_attention_ref[...]

    def remote(src, dst, send, recv, device):
        return pltpu.make_async_remote_copy(
            src_ref=src,
            dst_ref=dst,
            send_sem=send,
            recv_sem=recv,
            device_id=device,
            device_id_type=pl.DeviceIdType.MESH,
        )

    def x_copy(s):
        return remote(
            tsend.at[in_frame(1 - side, s)], xin.at[in_part(s)], x_send.at[s], x_recv.at[s], at_tm(partner)
        )

    def x_halo():
        return remote(tsend.at[edge_row], xin.at[halo], x_send.at[n_frame], x_recv.at[n_frame], at_tm(partner))

    def noise_copy():
        return remote(
            noise_ref.at[aligned(far_start, part)], noises.at[side], m_send.at[0], m_recv.at[0], at_tm(partner)
        )

    def noise_arrival():
        return remote(
            noise_ref.at[aligned(far_start, part)], noises.at[1 - side], m_send.at[0], m_recv.at[0], at_tm(partner)
        )

    def params_copy(to):
        return remote(params.at[side], params.at[to], m_send.at[1], m_recv.at[1], at_tm(partner))

    def f_copy(s):
        return remote(fsend.at[in_part(s)], fin.at[in_part(s)], f_send.at[s], f_recv.at[s], at_tm(partner))

    def z_copy(turn, i, rows):
        return remote(
            zout.at[turn, rows], zin.at[turn, rows], z_send.at[turn, i], z_recv.at[turn, i], at_tm(me_tm + 2)
        )

    for turn in range(ITERS):
        last = turn == ITERS - 1

        def in_copy(s, g):
            return remote(
                ain.at[turn, g, s], rin.at[turn, g, s], in_send.at[turn, g, s], in_recv.at[turn, g, s], at_frame(peer(s))
            )

        def out_copy(s, g):
            return remote(
                aout.at[turn, g, s],
                rout.at[turn, g, s],
                out_send.at[turn, g, s],
                out_recv.at[turn, g, s],
                at_frame(sender(s)),
            )

        def group(g):
            return (1 - side if g == 0 else side) if turn == 0 else g

        def near_rows(g, s, r):
            if turn == 0:
                return taps[pl.ds(pl.multiple_of(group(g) * part + peer(s) * piece + r * width, width), piece), :]
            return taps_two[g, pl.ds(pl.multiple_of(peer(s) * piece + r * width, width), piece), :]

        def mix(g, slots):
            near = [jnp.concatenate([near_rows(g, s, r) for r in range(3)], axis=1) for s in slots]
            total = jnp.dot(jnp.concatenate(near, axis=0), wconv_ref[...], preferred_element_type=f32)
            if turn == 0:
                here = [guess_ref[in_frame(group(g), s), :] for s in slots]
                noise = [noise_ref[in_frame(group(g), s), :] for s in slots]
                scale, value_of_time = coefficient, time_value
            else:
                here = [states[g, in_part(s), :] for s in slots]
                noise = [noises[g, in_part(s), :] for s in slots]
                scale, value_of_time = params[g, 2:3, :], params[g, 3:4, :]
            value = jnp.concatenate(here, axis=0) + total * (0.5 + 0.5 * jnp.tanh(0.5 * total))
            normed = (value * inverse_rms(value) * gain_attention).astype(bf16)
            for k, s in enumerate(slots):
                ain[turn, g, s] = normed[k * piece : (k + 1) * piece]
            for s in slots:
                if s != last_slot:
                    in_copy(s, g).start()
            for k, s in enumerate(slots):
                base[g, s] = scale * (value[k * piece : (k + 1) * piece] + value_of_time * noise[k])

        def project(g, blocks, slots):
            result = jnp.dot(jnp.concatenate(blocks, axis=0), wattn_ref[...], preferred_element_type=f32).astype(bf16)
            for k, s in enumerate(slots):
                proj[g, s] = result[k * piece : (k + 1) * piece]

        def attend(g):
            for b in range(piece // block):
                rows = slice(b * block, (b + 1) * block)
                query, key, value = (
                    jnp.concatenate([proj[g, s, rows, k * channels : (k + 1) * channels] for s in range(n_frame)], axis=0)
                    for k in range(3)
                )
                by_head = jnp.concatenate([query * heads_of[h : h + 1, :] for h in range(heads)], axis=0)
                scores = lax.dot_general(by_head, key, (((1,), (1,)), ((), ())), preferred_element_type=f32)
                scores = scores * (1.0 / math.sqrt(HEAD_DIM)) + jnp.concatenate([same_cell[...]] * heads, axis=0)
                raised = jnp.exp(scores - jnp.max(scores, axis=-1, keepdims=True))
                weights = (raised * (1.0 / jnp.sum(raised, axis=-1, keepdims=True))).astype(bf16)
                result = jnp.dot(weights, value, preferred_element_type=f32)
                size = n_frame * block
                mixed_heads = result[:size]
                for h in range(1, heads):
                    mixed_heads = jnp.where(head_lane == h, result[h * size : (h + 1) * size], mixed_heads)
                for s in range(n_frame):
                    aout[turn, g, s, rows, :] = mixed_heads[s * block : (s + 1) * block].astype(bf16)
            for s in others:
                out_copy(s, g).start()

        def close(g, blocks, slots):
            result = jnp.dot(jnp.concatenate(blocks, axis=0), wout_ref[...], preferred_element_type=f32)
            scale = coefficient if turn == 0 else params[g, 2:3, :]
            for k, s in enumerate(slots):
                value = base[g, s] + scale * result[k * piece : (k + 1) * piece]
                if turn == 0:
                    term[in_frame(group(g), s), :] = value
                    tsend[in_frame(group(g), s), :] = value.astype(bf16)
                else:
                    term_two[g, s] = value
            if turn == 0 and g == 0:
                for s in slots:
                    x_copy(s).start()
            if last and g == GROUPS - 1:
                settle(slots)

        def settle(slots):
            for s in slots:
                @pl.when(has_prev)
                def _():
                    z_copy(turn, s, in_part(s)).wait_recv()

                first = zin[turn, in_part(s), :].astype(f32) + term_two[0, s]
                second = first + term_two[1, s]
                zout[turn, in_part(s), :] = second.astype(bf16)
                fsend[in_part(s), :] = jnp.where(side == 0, second, first).astype(bf16)
                f_copy(s).start()

                @pl.when(has_next)
                def _():
                    z_copy(turn, s, in_part(s)).start()

                mine = in_frame(side, s)
                out_ref[mine, :] = start_ref[mine, :] + jnp.where(side == 0, first, second)

        for g in range(GROUPS):
            if turn == 0 and g == 0:
                meet()
            mix(g, far_slots)
        for g in range(GROUPS):
            mix(g, near_slots)
        if turn == 0:
            params_copy(side).start()
            noise_copy().start()
            for copy in loads[7:]:
                copy.wait()
        for g in range(GROUPS):
            project(g, [ain[turn, g, last_slot]], [last_slot])
        for g in range(GROUPS):
            for s in reversed(others):
                in_copy(s, g).wait_recv()
            project(g, [rin[turn, g, s] for s in others], others)
            attend(g)
        for g in range(GROUPS):
            close(g, [aout[turn, g, last_slot]], [last_slot])
            for s in others:
                in_copy(s, g).wait_send()
        for g in range(GROUPS):
            for s in reversed(others):
                out_copy(s, g).wait_recv()
            close(g, [rout[turn, g, s] for s in others], others)

        if not last:
            x_halo().start()

            def chain(i, rows, nat):
                z_copy_i = z_copy(turn, i, rows)

                @pl.when(has_prev)
                def _():
                    z_copy_i.wait_recv()

                total = zin[turn, rows, :].astype(f32) + (term[nat, :] + xin[rows, :].astype(f32))
                zout[turn, rows, :] = total.astype(bf16)
                z_copy_i.start()

            def chain_slot(s, _):
                x_copy(s).wait_recv()
                chain(s, in_part(s), in_frame(side, s))
                return 0

            @pl.when(has_next)
            def _():
                lax.fori_loop(0, n_frame, chain_slot, 0)
                x_halo().wait_recv()
                chain(n_frame, halo, halo_row)

            for g in range(GROUPS):
                for s in others:
                    out_copy(s, g).wait_send()
            params_copy(1 - side).wait_recv()
            noise_arrival().wait_recv()
            noise_copy().wait_send()
            params_copy(side).wait_send()

            def begin(i, rows, nat, arrival, at, keep):
                @pl.when(jnp.logical_not(has_next))
                def _():
                    arrival.wait_recv()

                    @pl.when(has_prev)
                    def _():
                        z_copy(turn, i, rows).wait_recv()

                first = start_ref[nat, :] + zin[turn, rows, :].astype(f32)
                second = first + jnp.where(side == 0, term[nat, :], xin[rows, :].astype(f32))
                for g, x in enumerate((first, second)):
                    if keep:
                        states[g, rows, :] = x

                    def put(columns, value):
                        taps_two[g, pl.ds(pl.multiple_of(at, width), x.shape[0]), columns] = value

                    make_taps(x, params[g, 0:1, :], params[g, 1:2, :], put)

            def begin_slot(s, _):
                begin(s, in_part(s), in_frame(side, s), x_copy(s), peer(s) * piece + width, True)
                return 0

            lax.fori_loop(0, n_frame, begin_slot, 0)
            begin(n_frame, halo, halo_row, x_halo(), (1 - side) * (part + width), False)

            def sent(s, _):
                x_copy(s).wait_send()

                @pl.when(has_next)
                def _():
                    z_copy(turn, s, in_part(s)).wait_send()

                return 0

            lax.fori_loop(0, n_frame, sent, 0)
            x_halo().wait_send()

            @pl.when(has_next)
            def _():
                z_copy(turn, n_frame, halo).wait_send()

    def receive(s, _):
        f_copy(s).wait_recv()
        rows = in_frame(1 - side, s)
        out_ref[rows, :] = start_ref[rows, :] + fin[in_part(s), :].astype(f32)
        return 0

    lax.fori_loop(0, n_frame, receive, 0)

    def sent_last(s, _):
        f_copy(s).wait_send()

        @pl.when(has_next)
        def _():
            z_copy(ITERS - 1, s, in_part(s)).wait_send()

        return 0

    lax.fori_loop(0, n_frame, sent_last, 0)
    for g in range(GROUPS):
        for s in others:
            remote(
                aout.at[ITERS - 1, g, s],
                rout.at[ITERS - 1, g, s],
                out_send.at[ITERS - 1, g, s],
                out_recv.at[ITERS - 1, g, s],
                at_frame(sender(s)),
            ).wait_send()


def shards(
    n_tm,
    n_frame,
    start_state,
    initial_guess,
    noise_draws,
    timesteps,
    gain_space,
    gain_attention,
    time_weight,
    space_weight,
    attention_weight,
    output_weight,
):
    _, height, width, channels = start_state.shape
    cells = height * width
    part = cells // 2
    piece = part // n_frame
    block = min(max(16, 128 // n_frame), piece)
    half_width = channels // 2
    frequency = np.exp(-math.log(10000.0) * np.arange(half_width) / half_width).astype(np.float32)
    frequency = np.concatenate([frequency, frequency])[None]
    f32, bf16 = jnp.float32, jnp.bfloat16
    dma, vmem = pltpu.SemaphoreType.DMA, pltpu.VMEM
    field = vmem((cells, channels), f32)
    row = vmem((1, channels), f32)
    exchange = vmem((ITERS, GROUPS, n_frame, piece, channels), bf16)
    carried = vmem((ITERS, part + width, channels), bf16)
    anywhere = pl.BlockSpec(memory_space=pl.ANY)
    total = pl.pallas_call(
        functools.partial(kernel, n_tm, n_frame, width),
        out_shape=pltpu.VMEM((cells, channels), f32),
        in_specs=[pl.BlockSpec(memory_space=pltpu.SMEM)] + [anywhere] * 10,
        out_specs=pl.BlockSpec(memory_space=pltpu.VMEM),
        scratch_shapes=[
            field,
            field,
            field,
            row,
            row,
            row,
            vmem(time_weight.shape, f32),
            vmem(space_weight.shape, bf16),
            vmem(attention_weight.shape, bf16),
            vmem(output_weight.shape, bf16),
            vmem((n_frame * block, n_frame * block), f32),
            vmem((2, 8, channels), f32),
            vmem((2, part, channels), f32),
            vmem((2, part, channels), f32),
            vmem((cells + 2 * width, 3 * channels), bf16),
            vmem((2, part + 2 * width, 3 * channels), bf16),
            vmem((GROUPS, n_frame, piece, channels), f32),
            field,
            vmem((GROUPS, n_frame, piece, channels), f32),
            vmem((GROUPS, n_frame, piece, 3 * channels), bf16),
            exchange,
            exchange,
            exchange,
            exchange,
            vmem((cells, channels), bf16),
            vmem((part + width, channels), bf16),
            carried,
            carried,
            vmem((part, channels), bf16),
            vmem((part, channels), bf16),
            dma((11,)),
            *([dma((ITERS, GROUPS, n_frame))] * 4),
            *([dma((n_frame + 1,))] * 2),
            *([dma((ITERS, n_frame + 1))] * 2),
            *([dma((n_frame,))] * 2),
            *([dma((2,))] * 2),
        ],
        compiler_params=pltpu.CompilerParams(collective_id=0, has_side_effects=True),
    )(
        timesteps,
        start_state.reshape(cells, channels),
        initial_guess.reshape(cells, channels),
        noise_draws.reshape(cells, channels),
        jnp.asarray(frequency),
        gain_space[None],
        gain_attention[None],
        time_weight,
        space_weight,
        attention_weight,
        output_weight,
    )
    return total.reshape(1, 1, height, width, channels)


def solution(mesh):
    return jax.shard_map(
        functools.partial(shards, mesh.shape["tm"], mesh.shape["frame"]),
        mesh=mesh,
        in_specs=(
            P("frame", None, None, None),
            P("tm", "frame", None, None, None),
            P("tm", "frame", None, None, None),
            P("tm"),
            P(),
            P(),
            P(),
            P(),
            P(),
            P(),
        ),
        out_specs=P("tm", "frame", None, None, None),
        check_vma=False,
    )
```

```python
import functools
import math

import jax
import jax.numpy as jnp
import numpy as np
from jax import lax
from jax.experimental import pallas as pl
from jax.experimental.pallas import tpu as pltpu
from jax.sharding import PartitionSpec as P

HEAD_DIM = 64
ITERS = 2
GROUPS = 2
EPS = 1e-06


def kernel(
    n_tm,
    n_frame,
    width,
    step_ref,
    start_hbm,
    guess_hbm,
    noise_hbm,
    freq_hbm,
    gain_space_hbm,
    gain_attention_hbm,
    wtime_hbm,
    wconv_hbm,
    wattn_hbm,
    wout_hbm,
    out_ref,
    start_ref,
    guess_ref,
    noise_ref,
    freq_ref,
    gain_space_ref,
    gain_attention_ref,
    wtime_ref,
    wconv_ref,
    wattn_ref,
    wout_ref,
    same_cell,
    params,
    noises,
    states,
    taps,
    taps_two,
    base,
    term,
    proj,
    ain,
    rin,
    aout,
    rout,
    msend,
    xin,
    other,
    nsend,
    hsend,
    hin,
    zin,
    zout,
    fsend,
    fin,
    load,
    in_send,
    in_recv,
    out_send,
    out_recv,
    x_send,
    x_recv,
    z_send,
    z_recv,
    f_send,
    f_recv,
    m_send,
    m_recv,
    h_send,
    h_recv,
    o_send,
    o_recv,
):
    cells, channels = start_hbm.shape
    part = cells // 2
    piece = part // n_frame
    part_rows = part // width
    sub = piece // GROUPS
    chips = n_frame // 2
    heads = channels // HEAD_DIM
    block = min(max(16, 128 // n_frame), piece // GROUPS)
    f32, bf16 = jnp.float32, jnp.bfloat16
    me_tm = lax.axis_index("tm")
    me = lax.axis_index("frame")
    my_chip, my_core = me // 2, lax.rem(me, 2)
    link, side = me_tm // 2, lax.rem(me_tm, 2)
    links = n_tm // 2
    has_prev = link > 0
    has_next = link < links - 1
    partner = me_tm + 1 - 2 * side

    last_slot = n_frame - 1
    far_slots = list(range(n_frame - 2))
    near_slots = [n_frame - 2, last_slot]
    others = list(range(last_slot))

    def peer(s):
        chip = lax.rem(my_chip + 1 + lax.div(s, 2), chips)
        return 2 * chip + lax.rem(my_core + s + lax.div(s + 2, n_frame), 2)

    def sender(s):
        chip = lax.rem(my_chip + 2 * chips - 1 - lax.div(s, 2), chips)
        return 2 * chip + lax.rem(my_core + s + lax.div(s + 2, n_frame), 2)

    def at_frame(f):
        return {"tm": me_tm, "frame": f}

    def at_tm(t):
        return {"tm": t, "frame": me}

    def aligned(n, size):
        return pl.ds(pl.multiple_of(n, size), size)

    def in_part(s):
        return aligned(peer(s) * piece, piece)

    def in_frame(h, s):
        return aligned(h * part + peer(s) * piece, piece)

    def sub_part(g, s):
        return aligned(peer(s) * piece + g * sub, sub)

    def sub_frame(h, g, s):
        return aligned(h * part + peer(s) * piece + g * sub, sub)

    own_start, far_start = side * part, (1 - side) * part
    edge_row = aligned((part_rows - 1 + side) * width, width)
    halo_row = aligned((part_rows - side) * width, width)
    halo = pl.ds(part, width)

    barrier = pltpu.get_barrier_semaphore()

    def greet(device):
        pl.semaphore_signal(barrier, inc=1, device_id=device, device_id_type=pl.DeviceIdType.MESH)

    for s in others:
        greet(at_frame(peer(s)))
    for s in range(n_frame):
        greet({"tm": partner, "frame": peer(s)})

    @pl.when(has_prev)
    def _():
        greet(at_tm(me_tm - 2))

    def meet():
        pl.semaphore_wait(barrier, 2 * n_frame - 1 + has_next.astype(jnp.int32))

    pairs = [
        (freq_hbm, freq_ref),
        (gain_space_hbm, gain_space_ref),
        (wtime_hbm, wtime_ref),
        (guess_hbm, guess_ref),
        (wconv_hbm, wconv_ref),
        (gain_attention_hbm, gain_attention_ref),
        (noise_hbm, noise_ref),
        (wattn_hbm, wattn_ref),
        (wout_hbm, wout_ref),
        (start_hbm, start_ref),
    ]
    loads = [pltpu.make_async_copy(src, dst, load.at[i]) for i, (src, dst) in enumerate(pairs)]
    for copy in loads:
        copy.start()

    edge = jnp.zeros((width, 3 * channels), bf16)
    taps[0:width, :] = edge
    taps[cells + width : cells + 2 * width, :] = edge
    for g in range(2):
        taps_two[g, aligned(side * (part + width), width), :] = edge

    @pl.when(jnp.logical_not(has_prev))
    def _():
        zin[...] = jnp.zeros_like(zin)

    row = lax.broadcasted_iota(jnp.int32, (n_frame * block, n_frame * block), 0)
    lane = lax.broadcasted_iota(jnp.int32, (n_frame * block, n_frame * block), 1)
    same_cell[...] = jnp.where(row % block == lane % block, 0.0, -jnp.inf)
    head_lane = lax.broadcasted_iota(jnp.int32, (n_frame * block, channels), 1) // HEAD_DIM
    heads_of = jnp.where(
        lax.broadcasted_iota(jnp.int32, (8, channels), 0) == lax.broadcasted_iota(jnp.int32, (8, channels), 1) // HEAD_DIM,
        1.0,
        0.0,
    ).astype(bf16)

    for copy in loads[:3]:
        copy.wait()
    step = jnp.full((8, channels), step_ref[0].astype(f32))
    time_value = step[0:1, :] / 1000.0
    coefficient = (0.5 + time_value) / math.sqrt(n_tm)
    angles = step * freq_ref[...]
    position = lax.broadcasted_iota(jnp.int32, (8, channels), 1)
    encoded = jnp.where(position < channels // 2, jnp.cos(angles), jnp.sin(angles))
    shifted = jnp.dot(encoded, wtime_ref[...], precision=lax.Precision.HIGHEST, preferred_element_type=f32)
    gain_space = gain_space_ref[...] * (1.0 + shifted[0:1, :channels])
    offset = shifted[0:1, channels:]
    for k, value in enumerate((gain_space, offset, coefficient, time_value)):
        params[side, k : k + 1, :] = value

    def inverse_rms(v):
        return lax.rsqrt(jnp.mean(v * v, axis=-1, keepdims=True) + EPS)

    def make_taps(x, gain, shift, put):
        rows = x.shape[0]
        column = lax.broadcasted_iota(jnp.int32, x.shape, 0) % width
        normed = x * inverse_rms(x) * gain + shift
        left = jnp.where(column == 0, 0.0, pltpu.roll(normed, 1, 0))
        right = jnp.where(column == width - 1, 0.0, pltpu.roll(normed, rows - 1, 0))
        for k, value in enumerate((left, normed, right)):
            put(slice(k * channels, (k + 1) * channels), value.astype(bf16))

    def first_taps(i, _):
        at = i * piece

        def put(columns, value):
            taps[pl.ds(pl.multiple_of(at + width, width), piece), columns] = value

        make_taps(guess_ref[aligned(at, piece), :], gain_space, offset, put)
        return 0

    loads[3].wait()
    lax.fori_loop(0, 2 * n_frame, first_taps, 0)
    for copy in loads[4:7]:
        copy.wait()
    gain_attention = gain_attention_ref[...]

    def remote(src, dst, send, recv, device):
        return pltpu.make_async_remote_copy(
            src_ref=src,
            dst_ref=dst,
            send_sem=send,
            recv_sem=recv,
            device_id=device,
            device_id_type=pl.DeviceIdType.MESH,
        )

    def x_copy(g, s):
        return remote(
            msend.at[sub_frame(1 - side, g, s)], xin.at[sub_part(g, s)], x_send.at[g, s], x_recv.at[g, s], at_tm(partner)
        )

    def x_halo():
        return remote(msend.at[edge_row], xin.at[halo], x_send.at[0, n_frame], x_recv.at[0, n_frame], at_tm(partner))

    behind_owner, edge_owner = side * last_slot, (1 - side) * last_slot

    def behind_copy(s):
        return remote(hsend.at[0, s], hin.at[0], h_send.at[0, s], h_recv.at[0], at_frame(sender(s)))

    def edge_copy(s):
        return remote(
            hsend.at[1, s], hin.at[1], h_send.at[1, s], h_recv.at[1], {"tm": partner, "frame": sender(s)}
        )

    def cut_row(k, s, behind):
        rows = jnp.concatenate([aout[0, g, s, k * sub : (k + 1) * sub, :] for g in range(GROUPS)], axis=0)
        return jnp.where(behind == 0, rows[:width], rows[piece - width :])

    def noise_copy():
        return remote(
            nsend, noises.at[side], m_send.at[0], m_recv.at[0], at_tm(partner)
        )

    def noise_arrival():
        return remote(
            nsend, noises.at[1 - side], m_send.at[0], m_recv.at[0], at_tm(partner)
        )

    def params_copy(to):
        return remote(params.at[side], params.at[to], m_send.at[1], m_recv.at[1], at_tm(partner))

    def f_copy(g, s):
        return remote(
            fsend.at[sub_part(g, s)], fin.at[sub_part(g, s)], f_send.at[g, s], f_recv.at[g, s], at_tm(partner)
        )

    def z_copy(turn, g, s, rows):
        return remote(
            zout.at[turn, rows], zin.at[turn, rows], z_send.at[turn, g, s], z_recv.at[turn, g, s], at_tm(me_tm + 2)
        )

    for turn in range(ITERS):
        last = turn == ITERS - 1

        def in_copy(s, g):
            return remote(
                ain.at[turn, g, s], rin.at[turn, g, s], in_send.at[turn, g, s], in_recv.at[turn, g, s], at_frame(peer(s))
            )

        def out_copy(s, g):
            rows = pl.ds(sub, sub) if turn == 0 else pl.ds(0, piece)
            return remote(
                aout.at[turn, g, s, rows],
                rout.at[turn, g, s, rows],
                out_send.at[turn, g, s],
                out_recv.at[turn, g, s],
                at_frame(sender(s)),
            )

        def over_copy(s, g):
            return remote(
                aout.at[0, g, s, pl.ds(0, sub)],
                rout.at[0, g, s, pl.ds(0, sub)],
                o_send.at[g, s],
                o_recv.at[g, s],
                {"tm": partner, "frame": sender(s)},
            )

        def frame_part(k):
            return 1 - side if k == 0 else side

        def near_rows(k, g, s, r):
            at = peer(s) * piece + g * sub + r * width
            if turn == 0:
                return taps[pl.ds(pl.multiple_of(frame_part(k) * part + at, 16), sub), :]
            return taps_two[k, pl.ds(pl.multiple_of(at, 16), sub), :]

        def mix(g, slots):
            each = [(s, k) for s in slots for k in range(2)]
            near = [jnp.concatenate([near_rows(k, g, s, r) for r in range(3)], axis=1) for s, k in each]
            total = jnp.dot(jnp.concatenate(near, axis=0), wconv_ref[...], preferred_element_type=f32)
            if turn == 0:
                here = [guess_ref[sub_frame(frame_part(k), g, s), :] for s, k in each]
            else:
                here = [states[k, sub_part(g, s), :] for s, k in each]
            value = jnp.concatenate(here, axis=0) + total * (0.5 + 0.5 * jnp.tanh(0.5 * total))
            normed = (value * inverse_rms(value) * gain_attention).astype(bf16)
            for i, s in enumerate(slots):
                ain[turn, g, s] = normed[i * piece : (i + 1) * piece]
            for s in slots:
                if s != last_slot:
                    in_copy(s, g).start()
            for i, (s, k) in enumerate(each):
                mine = value[i * sub : (i + 1) * sub]
                if turn == 0:
                    rows = sub_frame(frame_part(k), g, s)
                    known = coefficient * (mine + time_value * noise_ref[rows, :])
                    term[rows, :] = known
                    msend[rows, :] = known.astype(bf16)
                    if k == 0:
                        x_copy(g, s).start()
                else:
                    noise = noises[k, sub_part(g, s), :].astype(f32)
                    base[g, s, k * sub : (k + 1) * sub] = params[k, 2:3, :] * (mine + params[k, 3:4, :] * noise)

        def project(g, blocks, slots):
            result = jnp.dot(jnp.concatenate(blocks, axis=0), wattn_ref[...], preferred_element_type=f32).astype(bf16)
            for k, s in enumerate(slots):
                proj[g, s] = result[k * piece : (k + 1) * piece]

        def attend(g):
            for b in range(piece // block):
                rows = slice(b * block, (b + 1) * block)
                query, key, value = (
                    jnp.concatenate([proj[g, s, rows, k * channels : (k + 1) * channels] for s in range(n_frame)], axis=0)
                    for k in range(3)
                )
                by_head = jnp.concatenate([query * heads_of[h : h + 1, :] for h in range(heads)], axis=0)
                scores = lax.dot_general(by_head, key, (((1,), (1,)), ((), ())), preferred_element_type=f32)
                scores = scores * (1.0 / math.sqrt(HEAD_DIM)) + jnp.concatenate([same_cell[...]] * heads, axis=0)
                raised = jnp.exp(scores - jnp.max(scores, axis=-1, keepdims=True))
                weights = (raised * (1.0 / jnp.sum(raised, axis=-1, keepdims=True))).astype(bf16)
                result = jnp.dot(weights, value, preferred_element_type=f32)
                size = n_frame * block
                mixed_heads = result[:size]
                for h in range(1, heads):
                    mixed_heads = jnp.where(head_lane == h, result[h * size : (h + 1) * size], mixed_heads)
                for s in range(n_frame):
                    aout[turn, g, s, rows, :] = mixed_heads[s * block : (s + 1) * block].astype(bf16)
            for s in range(n_frame):
                if turn == 0:
                    over_copy(s, g).start()
                if s != last_slot:
                    out_copy(s, g).start()

        def close(g, blocks, slots):
            result = jnp.dot(jnp.concatenate(blocks, axis=0), wout_ref[...], preferred_element_type=f32)
            for i, s in enumerate(slots):
                first, second = result[i * piece : i * piece + sub], result[i * piece + sub : (i + 1) * piece]
                if turn == 0:
                    other[sub_part(g, s), :] = xin[sub_part(g, s), :].astype(f32) + params[1 - side, 2:3, :] * first
                    term[sub_frame(side, g, s), :] += coefficient * second
                else:
                    base[g, s, 0:sub] += params[0, 2:3, :] * first
                    base[g, s, sub:piece] += params[1, 2:3, :] * second

        def settle(g, slots):
            for s in slots:
                rows = sub_part(g, s)

                @pl.when(has_prev)
                def _():
                    z_copy(turn, g, s, rows).wait_recv()

                first = zin[turn, rows, :].astype(f32) + base[g, s, 0:sub]
                second = first + base[g, s, sub:piece]
                zout[turn, rows, :] = second.astype(bf16)
                fsend[rows, :] = jnp.where(side == 0, second, first).astype(bf16)
                f_copy(g, s).start()

                @pl.when(has_next)
                def _():
                    z_copy(turn, g, s, rows).start()

                mine = sub_frame(side, g, s)
                out_ref[mine, :] = start_ref[mine, :] + jnp.where(side == 0, first, second)

        def chain(g, s, rows, nat):
            @pl.when(has_prev)
            def _():
                z_copy(turn, g, s, rows).wait_recv()

            total = zin[turn, rows, :].astype(f32) + (term[nat, :] + other[rows, :])
            zout[turn, rows, :] = total.astype(bf16)
            z_copy(turn, g, s, rows).start()

        for g in range(GROUPS):
            if turn == 0 and g == 0:
                meet()
            mix(g, far_slots)
        if turn == 0:
            nsend[...] = noise_ref[aligned(far_start, part), :].astype(bf16)
            noise_copy().start()
        for g in range(GROUPS):
            mix(g, near_slots)
        if turn == 0:
            x_halo().start()
            params_copy(side).start()
            for copy in loads[7:]:
                copy.wait()
            noises[side] = noise_ref[aligned(own_start, part), :].astype(bf16)
        for g in range(GROUPS):
            project(g, [ain[turn, g, last_slot]], [last_slot])
        for g in range(GROUPS):
            for s in reversed(others):
                in_copy(s, g).wait_recv()
            project(g, [rin[turn, g, s] for s in others], others)
            attend(g)
        if turn == 0:

            @pl.when(me == behind_owner)
            def _():
                for s in others:
                    hsend[0, s] = cut_row(0, s, side)
                    behind_copy(s).start()
                hin[0] = cut_row(0, last_slot, side)

            @pl.when(me == edge_owner)
            def _():
                for s in range(n_frame):
                    hsend[1, s] = cut_row(1, s, 1 - side)
                    edge_copy(s).start()

            params_copy(1 - side).wait_recv()
        for g in range(GROUPS):
            for s in others:
                in_copy(s, g).wait_send()
        for g in range(GROUPS):
            if turn == 0:
                for s in range(n_frame):
                    x_copy(g, s).wait_recv()
                for s in reversed(range(n_frame)):
                    over_copy(s, g).wait_recv()
            else:
                close(g, [aout[turn, g, last_slot]], [last_slot])
                settle(g, [last_slot])
            for s in reversed(others):
                out_copy(s, g).wait_recv()
            if turn == 0:
                mine = jnp.concatenate([rout[0, g, last_slot, 0:sub, :], aout[0, g, last_slot, sub:piece, :]], axis=0)
                close(g, [rout[0, g, s] for s in others] + [mine], others + [last_slot])

                @pl.when(has_next)
                def _():
                    for s in range(n_frame):
                        chain(g, s, sub_part(g, s), sub_frame(side, g, s))

            else:
                close(g, [rout[turn, g, s] for s in others], others)
                settle(g, others)
        if turn == 0:

            @pl.when(me != behind_owner)
            def _():
                behind_copy(0).wait_recv()

            edge_copy(0).wait_recv()
            x_halo().wait_recv()
            beside = jnp.concatenate([hin[0], hin[1]], axis=0)
            result = jnp.dot(beside, wout_ref[...], preferred_element_type=f32)
            term[halo_row, :] += coefficient * result[:width]
            other[halo, :] = xin[halo, :].astype(f32) + params[1 - side, 2:3, :] * result[width:]

        if not last:

            @pl.when(has_next)
            def _():
                chain(0, n_frame, halo, halo_row)

            for g in range(GROUPS):
                for s in range(n_frame):
                    over_copy(s, g).wait_send()
                    if s != last_slot:
                        out_copy(s, g).wait_send()

            @pl.when(me == behind_owner)
            def _():
                for s in others:
                    behind_copy(s).wait_send()

            @pl.when(me == edge_owner)
            def _():
                for s in range(n_frame):
                    edge_copy(s).wait_send()

            noise_arrival().wait_recv()
            noise_copy().wait_send()
            params_copy(side).wait_send()

            def begin(rows, nat, at, keep):
                first = start_ref[nat, :] + zin[turn, rows, :].astype(f32)
                second = first + jnp.where(side == 0, term[nat, :], other[rows, :])
                for g, x in enumerate((first, second)):
                    if keep:
                        states[g, rows, :] = x

                    def put(columns, value):
                        taps_two[g, pl.ds(pl.multiple_of(at, width), x.shape[0]), columns] = value

                    make_taps(x, params[g, 0:1, :], params[g, 1:2, :], put)

            end_of_chain = jnp.logical_and(jnp.logical_not(has_next), has_prev)

            def begin_slot(s, _):
                @pl.when(end_of_chain)
                def _():
                    for g in range(GROUPS):
                        z_copy(turn, g, s, sub_part(g, s)).wait_recv()

                begin(in_part(s), in_frame(side, s), peer(s) * piece + width, True)
                return 0

            lax.fori_loop(0, n_frame, begin_slot, 0)

            @pl.when(end_of_chain)
            def _():
                z_copy(turn, 0, n_frame, halo).wait_recv()

            begin(halo, halo_row, (1 - side) * (part + width), False)

            def sent(s, _):
                for g in range(GROUPS):
                    x_copy(g, s).wait_send()

                    @pl.when(has_next)
                    def _():
                        z_copy(turn, g, s, sub_part(g, s)).wait_send()

                return 0

            lax.fori_loop(0, n_frame, sent, 0)
            x_halo().wait_send()

            @pl.when(has_next)
            def _():
                z_copy(turn, 0, n_frame, halo).wait_send()

    def receive(i, _):
        g, s = lax.div(i, n_frame), lax.rem(i, n_frame)
        f_copy(g, s).wait_recv()
        rows = sub_frame(1 - side, g, s)
        out_ref[rows, :] = start_ref[rows, :] + fin[sub_part(g, s), :].astype(f32)
        return 0

    lax.fori_loop(0, GROUPS * n_frame, receive, 0)

    def sent_last(i, _):
        g, s = lax.div(i, n_frame), lax.rem(i, n_frame)
        f_copy(g, s).wait_send()

        @pl.when(has_next)
        def _():
            z_copy(ITERS - 1, g, s, sub_part(g, s)).wait_send()

        return 0

    lax.fori_loop(0, GROUPS * n_frame, sent_last, 0)
    for g in range(GROUPS):
        for s in others:
            remote(
                aout.at[ITERS - 1, g, s],
                rout.at[ITERS - 1, g, s],
                out_send.at[ITERS - 1, g, s],
                out_recv.at[ITERS - 1, g, s],
                at_frame(sender(s)),
            ).wait_send()


def shards(
    n_tm,
    n_frame,
    start_state,
    initial_guess,
    noise_draws,
    timesteps,
    gain_space,
    gain_attention,
    time_weight,
    space_weight,
    attention_weight,
    output_weight,
):
    _, height, width, channels = start_state.shape
    cells = height * width
    part = cells // 2
    piece = part // n_frame
    block = min(max(16, 128 // n_frame), piece // GROUPS)
    half_width = channels // 2
    frequency = np.exp(-math.log(10000.0) * np.arange(half_width) / half_width).astype(np.float32)
    frequency = np.concatenate([frequency, frequency])[None]
    f32, bf16 = jnp.float32, jnp.bfloat16
    dma, vmem = pltpu.SemaphoreType.DMA, pltpu.VMEM
    field = vmem((cells, channels), f32)
    row = vmem((1, channels), f32)
    exchange = vmem((ITERS, GROUPS, n_frame, piece, channels), bf16)
    carried = vmem((ITERS, part + width, channels), bf16)
    anywhere = pl.BlockSpec(memory_space=pl.ANY)
    total = pl.pallas_call(
        functools.partial(kernel, n_tm, n_frame, width),
        out_shape=pltpu.VMEM((cells, channels), f32),
        in_specs=[pl.BlockSpec(memory_space=pltpu.SMEM)] + [anywhere] * 10,
        out_specs=pl.BlockSpec(memory_space=pltpu.VMEM),
        scratch_shapes=[
            field,
            field,
            field,
            row,
            row,
            row,
            vmem(time_weight.shape, f32),
            vmem(space_weight.shape, bf16),
            vmem(attention_weight.shape, bf16),
            vmem(output_weight.shape, bf16),
            vmem((n_frame * block, n_frame * block), f32),
            vmem((2, 8, channels), f32),
            vmem((2, part, channels), bf16),
            vmem((2, part, channels), f32),
            vmem((cells + 2 * width, 3 * channels), bf16),
            vmem((2, part + 2 * width, 3 * channels), bf16),
            vmem((GROUPS, n_frame, piece, channels), f32),
            field,
            vmem((GROUPS, n_frame, piece, 3 * channels), bf16),
            exchange,
            exchange,
            exchange,
            exchange,
            vmem((cells, channels), bf16),
            vmem((part + width, channels), bf16),
            vmem((part + width, channels), f32),
            vmem((part, channels), bf16),
            vmem((2, n_frame, width, channels), bf16),
            vmem((2, width, channels), bf16),
            carried,
            carried,
            vmem((part, channels), bf16),
            vmem((part, channels), bf16),
            dma((10,)),
            *([dma((ITERS, GROUPS, n_frame))] * 4),
            *([dma((GROUPS, n_frame + 1))] * 2),
            *([dma((ITERS, GROUPS, n_frame + 1))] * 2),
            *([dma((GROUPS, n_frame))] * 2),
            *([dma((2,))] * 2),
            dma((2, n_frame)),
            dma((2,)),
            *([dma((GROUPS, n_frame))] * 2),
        ],
        compiler_params=pltpu.CompilerParams(collective_id=0, has_side_effects=True),
    )(
        timesteps,
        start_state.reshape(cells, channels),
        initial_guess.reshape(cells, channels),
        noise_draws.reshape(cells, channels),
        jnp.asarray(frequency),
        gain_space[None],
        gain_attention[None],
        time_weight,
        space_weight,
        attention_weight,
        output_weight,
    )
    return total.reshape(1, 1, height, width, channels)


def solution(mesh):
    return jax.shard_map(
        functools.partial(shards, mesh.shape["tm"], mesh.shape["frame"]),
        mesh=mesh,
        in_specs=(
            P("frame", None, None, None),
            P("tm", "frame", None, None, None),
            P("tm", "frame", None, None, None),
            P("tm"),
            P(),
            P(),
            P(),
            P(),
            P(),
            P(),
        ),
        out_specs=P("tm", "frame", None, None, None),
        check_vma=False,
    )
```

```python
import functools
import math

import jax
import jax.numpy as jnp
import numpy as np
from jax import lax
from jax.experimental import pallas as pl
from jax.experimental.pallas import tpu as pltpu
from jax.sharding import PartitionSpec as P

HEAD_DIM = 64
ITERS = 2
GROUPS = 2
EPS = 1e-06


def kernel(
    n_tm,
    n_frame,
    width,
    groups,
    step_ref,
    start_hbm,
    guess_hbm,
    noise_hbm,
    freq_hbm,
    gain_space_hbm,
    gain_attention_hbm,
    wtime_hbm,
    wconv_hbm,
    wattn_hbm,
    wout_hbm,
    out_ref,
    start_ref,
    guess_ref,
    noise_ref,
    freq_ref,
    gain_space_ref,
    gain_attention_ref,
    wtime_ref,
    wconv_ref,
    wattn_ref,
    wout_ref,
    same_cell,
    params,
    noises,
    states,
    taps,
    taps_two,
    base,
    term,
    proj,
    ain,
    rin,
    aout,
    rout,
    msend,
    xin,
    other,
    nsend,
    hsend,
    hin,
    zin,
    zout,
    fsend,
    fin,
    load,
    in_send,
    in_recv,
    out_send,
    out_recv,
    x_send,
    x_recv,
    z_send,
    z_recv,
    f_send,
    f_recv,
    m_send,
    m_recv,
    h_send,
    h_recv,
    o_send,
    o_recv,
):
    cells, channels = start_hbm.shape
    part = cells // 2
    piece = part // n_frame
    part_rows = part // width
    sub = piece // groups
    unit = 2 * sub
    chips = n_frame // 2
    heads = channels // HEAD_DIM
    block = min(max(16, 128 // n_frame), piece // groups)
    f32, bf16 = jnp.float32, jnp.bfloat16
    me_tm = lax.axis_index("tm")
    me = lax.axis_index("frame")
    my_chip, my_core = me // 2, lax.rem(me, 2)
    link, side = me_tm // 2, lax.rem(me_tm, 2)
    links = n_tm // 2
    has_prev = link > 0
    has_next = link < links - 1
    partner = me_tm + 1 - 2 * side

    last_slot = n_frame - 1
    far_slots = list(range(n_frame - 2))
    near_slots = [n_frame - 2, last_slot]
    others = list(range(last_slot))

    def peer(s):
        chip = lax.rem(my_chip + 1 + lax.div(s, 2), chips)
        return 2 * chip + lax.rem(my_core + s + lax.div(s + 2, n_frame), 2)

    def sender(s):
        chip = lax.rem(my_chip + 2 * chips - 1 - lax.div(s, 2), chips)
        return 2 * chip + lax.rem(my_core + s + lax.div(s + 2, n_frame), 2)

    def at_frame(f):
        return {"tm": me_tm, "frame": f}

    def at_tm(t):
        return {"tm": t, "frame": me}

    def aligned(n, size):
        return pl.ds(pl.multiple_of(n, size), size)

    def in_part(s):
        return aligned(peer(s) * piece, piece)

    def in_frame(h, s):
        return aligned(h * part + peer(s) * piece, piece)

    def sub_part(g, s):
        return aligned(peer(s) * piece + g * sub, sub)

    def sub_frame(h, g, s):
        return aligned(h * part + peer(s) * piece + g * sub, sub)

    own_start, far_start = side * part, (1 - side) * part
    edge_row = aligned((part_rows - 1 + side) * width, width)
    halo_row = aligned((part_rows - side) * width, width)
    halo = pl.ds(part, width)

    barrier = pltpu.get_barrier_semaphore()

    def batches(size):
        return [list(range(groups))[g : g + size] for g in range(0, groups, size)]

    def greet(device):
        pl.semaphore_signal(barrier, inc=1, device_id=device, device_id_type=pl.DeviceIdType.MESH)

    for s in others:
        greet(at_frame(peer(s)))
    for s in range(n_frame):
        greet({"tm": partner, "frame": peer(s)})

    @pl.when(has_prev)
    def _():
        greet(at_tm(me_tm - 2))

    def meet():
        pl.semaphore_wait(barrier, 2 * n_frame - 1 + has_next.astype(jnp.int32))

    pairs = [
        (freq_hbm, freq_ref),
        (gain_space_hbm, gain_space_ref),
        (wtime_hbm, wtime_ref),
        (guess_hbm, guess_ref),
        (wconv_hbm, wconv_ref),
        (gain_attention_hbm, gain_attention_ref),
        (noise_hbm, noise_ref),
        (wattn_hbm, wattn_ref),
        (wout_hbm, wout_ref),
        (start_hbm, start_ref),
    ]
    loads = [pltpu.make_async_copy(src, dst, load.at[i]) for i, (src, dst) in enumerate(pairs)]
    for copy in loads:
        copy.start()

    edge = jnp.zeros((width, 3 * channels), bf16)
    taps[0:width, :] = edge
    taps[cells + width : cells + 2 * width, :] = edge
    for g in range(2):
        taps_two[g, aligned(side * (part + width), width), :] = edge

    @pl.when(jnp.logical_not(has_prev))
    def _():
        zin[...] = jnp.zeros_like(zin)

    row = lax.broadcasted_iota(jnp.int32, (n_frame * block, n_frame * block), 0)
    lane = lax.broadcasted_iota(jnp.int32, (n_frame * block, n_frame * block), 1)
    same_cell[...] = jnp.where(row % block == lane % block, 0.0, -jnp.inf)
    head_lane = lax.broadcasted_iota(jnp.int32, (n_frame * block, channels), 1) // HEAD_DIM
    heads_of = jnp.where(
        lax.broadcasted_iota(jnp.int32, (8, channels), 0) == lax.broadcasted_iota(jnp.int32, (8, channels), 1) // HEAD_DIM,
        1.0,
        0.0,
    ).astype(bf16)

    for copy in loads[:3]:
        copy.wait()
    step = jnp.full((8, channels), step_ref[0].astype(f32))
    time_value = step[0:1, :] / 1000.0
    coefficient = (0.5 + time_value) / math.sqrt(n_tm)
    angles = step * freq_ref[...]
    position = lax.broadcasted_iota(jnp.int32, (8, channels), 1)
    encoded = jnp.where(position < channels // 2, jnp.cos(angles), jnp.sin(angles))
    shifted = jnp.dot(encoded, wtime_ref[...], precision=lax.Precision.HIGHEST, preferred_element_type=f32)
    gain_space = gain_space_ref[...] * (1.0 + shifted[0:1, :channels])
    offset = shifted[0:1, channels:]
    for k, value in enumerate((gain_space, offset, coefficient, time_value)):
        params[side, k : k + 1, :] = value

    def inverse_rms(v):
        return lax.rsqrt(jnp.mean(v * v, axis=-1, keepdims=True) + EPS)

    def make_taps(x, gain, shift, put):
        rows = x.shape[0]
        column = lax.broadcasted_iota(jnp.int32, x.shape, 0) % width
        normed = x * inverse_rms(x) * gain + shift
        left = jnp.where(column == 0, 0.0, pltpu.roll(normed, 1, 0))
        right = jnp.where(column == width - 1, 0.0, pltpu.roll(normed, rows - 1, 0))
        for k, value in enumerate((left, normed, right)):
            put(slice(k * channels, (k + 1) * channels), value.astype(bf16))

    def first_taps(i, _):
        at = i * piece

        def put(columns, value):
            taps[pl.ds(pl.multiple_of(at + width, width), piece), columns] = value

        make_taps(guess_ref[aligned(at, piece), :], gain_space, offset, put)
        return 0

    loads[3].wait()
    lax.fori_loop(0, 2 * n_frame, first_taps, 0, unroll=4)
    for copy in loads[4:7]:
        copy.wait()
    gain_attention = gain_attention_ref[...]

    def remote(src, dst, send, recv, device):
        return pltpu.make_async_remote_copy(
            src_ref=src,
            dst_ref=dst,
            send_sem=send,
            recv_sem=recv,
            device_id=device,
            device_id_type=pl.DeviceIdType.MESH,
        )

    def x_copy(g, s):
        return remote(
            msend.at[sub_frame(1 - side, g, s)], xin.at[sub_part(g, s)], x_send.at[g, s], x_recv.at[g, s], at_tm(partner)
        )

    def x_halo():
        return remote(msend.at[edge_row], xin.at[halo], x_send.at[0, n_frame], x_recv.at[0, n_frame], at_tm(partner))

    behind_owner, edge_owner = side * last_slot, (1 - side) * last_slot

    def behind_copy(s):
        return remote(hsend.at[0, s], hin.at[0], h_send.at[0, s], h_recv.at[0], at_frame(sender(s)))

    def edge_copy(s):
        return remote(
            hsend.at[1, s], hin.at[1], h_send.at[1, s], h_recv.at[1], {"tm": partner, "frame": sender(s)}
        )

    def cut_row(k, s, behind):
        rows = jnp.concatenate([aout[0, g, s, k * sub : (k + 1) * sub, :] for g in range(groups)], axis=0)
        return jnp.where(behind == 0, rows[:width], rows[piece - width :])

    def noise_copy():
        return remote(
            nsend, noises.at[side], m_send.at[0], m_recv.at[0], at_tm(partner)
        )

    def noise_arrival():
        return remote(
            nsend, noises.at[1 - side], m_send.at[0], m_recv.at[0], at_tm(partner)
        )

    def params_copy(to):
        return remote(params.at[side], params.at[to], m_send.at[1], m_recv.at[1], at_tm(partner))

    def f_copy(g, s):
        return remote(
            fsend.at[sub_part(g, s)], fin.at[sub_part(g, s)], f_send.at[g, s], f_recv.at[g, s], at_tm(partner)
        )

    def z_copy(turn, g, s, rows):
        return remote(
            zout.at[turn, rows], zin.at[turn, rows], z_send.at[turn, g, s], z_recv.at[turn, g, s], at_tm(me_tm + 2)
        )

    for turn in range(ITERS):
        last = turn == ITERS - 1

        def in_copy(s, g):
            return remote(
                ain.at[turn, g, s], rin.at[turn, g, s], in_send.at[turn, g, s], in_recv.at[turn, g, s], at_frame(peer(s))
            )

        def out_copy(s, g):
            rows = pl.ds(sub, sub) if turn == 0 else pl.ds(0, unit)
            return remote(
                aout.at[turn, g, s, rows],
                rout.at[turn, g, s, rows],
                out_send.at[turn, g, s],
                out_recv.at[turn, g, s],
                at_frame(sender(s)),
            )

        def over_copy(s, g):
            return remote(
                aout.at[0, g, s, pl.ds(0, sub)],
                rout.at[0, g, s, pl.ds(0, sub)],
                o_send.at[g, s],
                o_recv.at[g, s],
                {"tm": partner, "frame": sender(s)},
            )

        def frame_part(k):
            return 1 - side if k == 0 else side

        def near_rows(k, g, s, r):
            at = peer(s) * piece + g * sub + r * width
            if turn == 0:
                return taps[pl.ds(pl.multiple_of(frame_part(k) * part + at, 16), sub), :]
            return taps_two[k, pl.ds(pl.multiple_of(at, 16), sub), :]

        def mix(gs, slots):
            each = [(g, s, k) for g in gs for s in slots for k in range(2)]
            near = [jnp.concatenate([near_rows(k, g, s, r) for r in range(3)], axis=1) for g, s, k in each]
            total = jnp.dot(jnp.concatenate(near, axis=0), wconv_ref[...], preferred_element_type=f32)
            if turn == 0:
                here = [guess_ref[sub_frame(frame_part(k), g, s), :] for g, s, k in each]
            else:
                here = [states[k, sub_part(g, s), :] for g, s, k in each]
            value = jnp.concatenate(here, axis=0) + total * (0.5 + 0.5 * jnp.tanh(0.5 * total))
            normed = (value * inverse_rms(value) * gain_attention).astype(bf16)
            for i, (g, s) in enumerate((g, s) for g in gs for s in slots):
                ain[turn, g, s] = normed[i * unit : (i + 1) * unit]
                if s != last_slot:
                    in_copy(s, g).start()
            for i, (g, s, k) in enumerate(each):
                mine = value[i * sub : (i + 1) * sub]
                if turn == 0:
                    rows = sub_frame(frame_part(k), g, s)
                    known = coefficient * (mine + time_value * noise_ref[rows, :])
                    term[rows, :] = known
                    msend[rows, :] = known.astype(bf16)
                    if k == 0:
                        x_copy(g, s).start()
                else:
                    noise = noises[k, sub_part(g, s), :].astype(f32)
                    base[g, s, k * sub : (k + 1) * sub] = params[k, 2:3, :] * (mine + params[k, 3:4, :] * noise)

        def project(g, blocks, slots):
            result = jnp.dot(jnp.concatenate(blocks, axis=0), wattn_ref[...], preferred_element_type=f32).astype(bf16)
            for k, s in enumerate(slots):
                proj[g, s] = result[k * unit : (k + 1) * unit]

        def attend(g):
            for b in range(unit // block):
                rows = slice(b * block, (b + 1) * block)
                query, key, value = (
                    jnp.concatenate([proj[g, s, rows, k * channels : (k + 1) * channels] for s in range(n_frame)], axis=0)
                    for k in range(3)
                )
                by_head = jnp.concatenate([query * heads_of[h : h + 1, :] for h in range(heads)], axis=0)
                scores = lax.dot_general(by_head, key, (((1,), (1,)), ((), ())), preferred_element_type=f32)
                scores = scores * (1.0 / math.sqrt(HEAD_DIM)) + jnp.concatenate([same_cell[...]] * heads, axis=0)
                raised = jnp.exp(scores - jnp.max(scores, axis=-1, keepdims=True))
                weights = (raised * (1.0 / jnp.sum(raised, axis=-1, keepdims=True))).astype(bf16)
                result = jnp.dot(weights, value, preferred_element_type=f32)
                size = n_frame * block
                mixed_heads = result[:size]
                for h in range(1, heads):
                    mixed_heads = jnp.where(head_lane == h, result[h * size : (h + 1) * size], mixed_heads)
                for s in range(n_frame):
                    aout[turn, g, s, rows, :] = mixed_heads[s * block : (s + 1) * block].astype(bf16)
            for s in range(n_frame):
                if turn == 0:
                    over_copy(s, g).start()
                if s != last_slot:
                    out_copy(s, g).start()

        def close(g, blocks, slots):
            result = jnp.dot(jnp.concatenate(blocks, axis=0), wout_ref[...], preferred_element_type=f32)
            for i, s in enumerate(slots):
                first, second = result[i * unit : i * unit + sub], result[i * unit + sub : (i + 1) * unit]
                if turn == 0:
                    other[sub_part(g, s), :] = xin[sub_part(g, s), :].astype(f32) + params[1 - side, 2:3, :] * first
                    term[sub_frame(side, g, s), :] += coefficient * second
                else:
                    base[g, s, 0:sub] += params[0, 2:3, :] * first
                    base[g, s, sub:unit] += params[1, 2:3, :] * second

        def settle(g, slots):
            for s in slots:
                rows = sub_part(g, s)

                @pl.when(has_prev)
                def _():
                    z_copy(turn, g, s, rows).wait_recv()

                first = zin[turn, rows, :].astype(f32) + base[g, s, 0:sub]
                second = first + base[g, s, sub:unit]
                zout[turn, rows, :] = second.astype(bf16)
                fsend[rows, :] = jnp.where(side == 0, second, first).astype(bf16)
                f_copy(g, s).start()

                @pl.when(has_next)
                def _():
                    z_copy(turn, g, s, rows).start()

                mine = sub_frame(side, g, s)
                out_ref[mine, :] = start_ref[mine, :] + jnp.where(side == 0, first, second)

        def chain(g, s, rows, nat):
            @pl.when(has_prev)
            def _():
                z_copy(turn, g, s, rows).wait_recv()

            total = zin[turn, rows, :].astype(f32) + (term[nat, :] + other[rows, :])
            zout[turn, rows, :] = total.astype(bf16)
            z_copy(turn, g, s, rows).start()

        if turn == 0:
            meet()
        for gs in batches(1):
            mix(gs, far_slots)
        if turn == 0:
            nsend[...] = noise_ref[aligned(far_start, part), :].astype(bf16)
            noise_copy().start()
        for gs in batches(1):
            mix(gs, near_slots)
        if turn == 0:
            x_halo().start()
            params_copy(side).start()
            for copy in loads[7:]:
                copy.wait()
            noises[side] = noise_ref[aligned(own_start, part), :].astype(bf16)
        for g in range(groups):
            project(g, [ain[turn, g, last_slot]], [last_slot])
        for g in range(groups):
            for s in reversed(others):
                in_copy(s, g).wait_recv()
            project(g, [rin[turn, g, s] for s in others], others)
            attend(g)
        if turn == 0:

            @pl.when(me == behind_owner)
            def _():
                for s in others:
                    hsend[0, s] = cut_row(0, s, side)
                    behind_copy(s).start()
                hin[0] = cut_row(0, last_slot, side)

            @pl.when(me == edge_owner)
            def _():
                for s in range(n_frame):
                    hsend[1, s] = cut_row(1, s, 1 - side)
                    edge_copy(s).start()

            params_copy(1 - side).wait_recv()
        for g in range(groups):
            for s in others:
                in_copy(s, g).wait_send()
        for g in range(groups):
            if turn == 0:
                for s in range(n_frame):
                    x_copy(g, s).wait_recv()
                for s in reversed(range(n_frame)):
                    over_copy(s, g).wait_recv()
            else:
                close(g, [aout[turn, g, last_slot]], [last_slot])
                settle(g, [last_slot])
            for s in reversed(others):
                out_copy(s, g).wait_recv()
            if turn == 0:
                mine = jnp.concatenate([rout[0, g, last_slot, 0:sub, :], aout[0, g, last_slot, sub:unit, :]], axis=0)
                close(g, [rout[0, g, s] for s in others] + [mine], others + [last_slot])

                @pl.when(has_next)
                def _():
                    for s in range(n_frame):
                        chain(g, s, sub_part(g, s), sub_frame(side, g, s))

            else:
                close(g, [rout[turn, g, s] for s in others], others)
                settle(g, others)
        if turn == 0:

            @pl.when(me != behind_owner)
            def _():
                behind_copy(0).wait_recv()

            edge_copy(0).wait_recv()
            x_halo().wait_recv()
            beside = jnp.concatenate([hin[0], hin[1]], axis=0)
            result = jnp.dot(beside, wout_ref[...], preferred_element_type=f32)
            term[halo_row, :] += coefficient * result[:width]
            other[halo, :] = xin[halo, :].astype(f32) + params[1 - side, 2:3, :] * result[width:]

        if not last:

            @pl.when(has_next)
            def _():
                chain(0, n_frame, halo, halo_row)

            for g in range(groups):
                for s in range(n_frame):
                    over_copy(s, g).wait_send()
                    if s != last_slot:
                        out_copy(s, g).wait_send()

            @pl.when(me == behind_owner)
            def _():
                for s in others:
                    behind_copy(s).wait_send()

            @pl.when(me == edge_owner)
            def _():
                for s in range(n_frame):
                    edge_copy(s).wait_send()

            noise_arrival().wait_recv()
            noise_copy().wait_send()
            params_copy(side).wait_send()

            def begin(rows, nat, at, keep):
                first = start_ref[nat, :] + zin[turn, rows, :].astype(f32)
                second = first + jnp.where(side == 0, term[nat, :], other[rows, :])
                for g, x in enumerate((first, second)):
                    if keep:
                        states[g, rows, :] = x

                    def put(columns, value):
                        taps_two[g, pl.ds(pl.multiple_of(at, width), x.shape[0]), columns] = value

                    make_taps(x, params[g, 0:1, :], params[g, 1:2, :], put)

            end_of_chain = jnp.logical_and(jnp.logical_not(has_next), has_prev)

            def begin_slot(s, _):
                @pl.when(end_of_chain)
                def _():
                    for g in range(groups):
                        z_copy(turn, g, s, sub_part(g, s)).wait_recv()

                begin(in_part(s), in_frame(side, s), peer(s) * piece + width, True)
                return 0

            lax.fori_loop(0, n_frame, begin_slot, 0, unroll=True)

            @pl.when(end_of_chain)
            def _():
                z_copy(turn, 0, n_frame, halo).wait_recv()

            begin(halo, halo_row, (1 - side) * (part + width), False)

            def sent(s, _):
                for g in range(groups):
                    x_copy(g, s).wait_send()

                    @pl.when(has_next)
                    def _():
                        z_copy(turn, g, s, sub_part(g, s)).wait_send()

                return 0

            lax.fori_loop(0, n_frame, sent, 0)
            x_halo().wait_send()

            @pl.when(has_next)
            def _():
                z_copy(turn, 0, n_frame, halo).wait_send()

    def receive(i, _):
        g, s = lax.div(i, n_frame), lax.rem(i, n_frame)
        f_copy(g, s).wait_recv()
        rows = sub_frame(1 - side, g, s)
        out_ref[rows, :] = start_ref[rows, :] + fin[sub_part(g, s), :].astype(f32)
        return 0

    lax.fori_loop(0, groups * n_frame, receive, 0)

    def sent_last(i, _):
        g, s = lax.div(i, n_frame), lax.rem(i, n_frame)
        f_copy(g, s).wait_send()

        @pl.when(has_next)
        def _():
            z_copy(ITERS - 1, g, s, sub_part(g, s)).wait_send()

        return 0

    lax.fori_loop(0, groups * n_frame, sent_last, 0)
    for g in range(groups):
        for s in others:
            remote(
                aout.at[ITERS - 1, g, s],
                rout.at[ITERS - 1, g, s],
                out_send.at[ITERS - 1, g, s],
                out_recv.at[ITERS - 1, g, s],
                at_frame(sender(s)),
            ).wait_send()


def shards(
    n_tm,
    n_frame,
    start_state,
    initial_guess,
    noise_draws,
    timesteps,
    gain_space,
    gain_attention,
    time_weight,
    space_weight,
    attention_weight,
    output_weight,
):
    _, height, width, channels = start_state.shape
    cells = height * width
    part = cells // 2
    piece = part // n_frame
    groups = min(GROUPS, piece // 16)
    block = min(max(16, 128 // n_frame), piece // groups)
    half_width = channels // 2
    frequency = np.exp(-math.log(10000.0) * np.arange(half_width) / half_width).astype(np.float32)
    frequency = np.concatenate([frequency, frequency])[None]
    f32, bf16 = jnp.float32, jnp.bfloat16
    dma, vmem = pltpu.SemaphoreType.DMA, pltpu.VMEM
    field = vmem((cells, channels), f32)
    row = vmem((1, channels), f32)
    exchange = vmem((ITERS, groups, n_frame, 2 * piece // groups, channels), bf16)
    carried = vmem((ITERS, part + width, channels), bf16)
    anywhere = pl.BlockSpec(memory_space=pl.ANY)
    total = pl.pallas_call(
        functools.partial(kernel, n_tm, n_frame, width, groups),
        out_shape=pltpu.VMEM((cells, channels), f32),
        in_specs=[pl.BlockSpec(memory_space=pltpu.SMEM)] + [anywhere] * 10,
        out_specs=pl.BlockSpec(memory_space=pltpu.VMEM),
        scratch_shapes=[
            field,
            field,
            field,
            row,
            row,
            row,
            vmem(time_weight.shape, f32),
            vmem(space_weight.shape, bf16),
            vmem(attention_weight.shape, bf16),
            vmem(output_weight.shape, bf16),
            vmem((n_frame * block, n_frame * block), f32),
            vmem((2, 8, channels), f32),
            vmem((2, part, channels), bf16),
            vmem((2, part, channels), f32),
            vmem((cells + 2 * width, 3 * channels), bf16),
            vmem((2, part + 2 * width, 3 * channels), bf16),
            vmem((groups, n_frame, 2 * piece // groups, channels), f32),
            field,
            vmem((groups, n_frame, 2 * piece // groups, 3 * channels), bf16),
            exchange,
            exchange,
            exchange,
            exchange,
            vmem((cells, channels), bf16),
            vmem((part + width, channels), bf16),
            vmem((part + width, channels), f32),
            vmem((part, channels), bf16),
            vmem((2, n_frame, width, channels), bf16),
            vmem((2, width, channels), bf16),
            carried,
            carried,
            vmem((part, channels), bf16),
            vmem((part, channels), bf16),
            dma((10,)),
            *([dma((ITERS, groups, n_frame))] * 4),
            *([dma((groups, n_frame + 1))] * 2),
            *([dma((ITERS, groups, n_frame + 1))] * 2),
            *([dma((groups, n_frame))] * 2),
            *([dma((2,))] * 2),
            dma((2, n_frame)),
            dma((2,)),
            *([dma((groups, n_frame))] * 2),
        ],
        compiler_params=pltpu.CompilerParams(collective_id=0, has_side_effects=True),
    )(
        timesteps,
        start_state.reshape(cells, channels),
        initial_guess.reshape(cells, channels),
        noise_draws.reshape(cells, channels),
        jnp.asarray(frequency),
        gain_space[None],
        gain_attention[None],
        time_weight,
        space_weight,
        attention_weight,
        output_weight,
    )
    return total.reshape(1, 1, height, width, channels)


def solution(mesh):
    return jax.shard_map(
        functools.partial(shards, mesh.shape["tm"], mesh.shape["frame"]),
        mesh=mesh,
        in_specs=(
            P("frame", None, None, None),
            P("tm", "frame", None, None, None),
            P("tm", "frame", None, None, None),
            P("tm"),
            P(),
            P(),
            P(),
            P(),
            P(),
            P(),
        ),
        out_specs=P("tm", "frame", None, None, None),
        check_vma=False,
    )
```

```python
import functools
import math

import jax
import jax.numpy as jnp
import numpy as np
from jax import lax
from jax.experimental import pallas as pl
from jax.experimental.pallas import tpu as pltpu
from jax.sharding import PartitionSpec as P

HEAD_DIM = 64
ITERS = 2
GROUPS = 2
EPS = 1e-06


def kernel(
    n_tm,
    n_frame,
    width,
    groups,
    step_ref,
    start_hbm,
    guess_hbm,
    noise_hbm,
    freq_hbm,
    gain_space_hbm,
    gain_attention_hbm,
    wtime_hbm,
    wconv_hbm,
    wattn_hbm,
    wout_hbm,
    out_ref,
    start_ref,
    guess_ref,
    noise_ref,
    freq_ref,
    gain_space_ref,
    gain_attention_ref,
    wtime_ref,
    wconv_ref,
    wattn_ref,
    wout_ref,
    same_cell,
    params,
    noises,
    states,
    taps,
    taps_two,
    base,
    term,
    proj,
    ain,
    rin,
    aout,
    rout,
    msend,
    xin,
    other,
    nsend,
    hsend,
    hin,
    zin,
    zout,
    fsend,
    fin,
    load,
    in_send,
    in_recv,
    out_send,
    out_recv,
    x_send,
    x_recv,
    z_send,
    z_recv,
    f_send,
    f_recv,
    m_send,
    m_recv,
    h_send,
    h_recv,
    o_send,
    o_recv,
):
    cells, channels = start_hbm.shape
    part = cells // 2
    piece = part // n_frame
    part_rows = part // width
    sub = piece // groups
    unit = 2 * sub
    chips = n_frame // 2
    heads = channels // HEAD_DIM
    block = min(max(16, 128 // n_frame), piece // groups)
    f32, bf16 = jnp.float32, jnp.bfloat16
    me_tm = lax.axis_index("tm")
    me = lax.axis_index("frame")
    my_chip, my_core = me // 2, lax.rem(me, 2)
    link, side = me_tm // 2, lax.rem(me_tm, 2)
    links = n_tm // 2
    has_prev = link > 0
    has_next = link < links - 1
    partner = me_tm + 1 - 2 * side

    last_slot = n_frame - 1
    far_slots = list(range(n_frame - 2))
    near_slots = [n_frame - 2, last_slot]
    others = list(range(last_slot))

    def peer(s):
        chip = lax.rem(my_chip + 1 + lax.div(s, 2), chips)
        return 2 * chip + lax.rem(my_core + s + lax.div(s + 2, n_frame), 2)

    def sender(s):
        chip = lax.rem(my_chip + 2 * chips - 1 - lax.div(s, 2), chips)
        return 2 * chip + lax.rem(my_core + s + lax.div(s + 2, n_frame), 2)

    def at_frame(f):
        return {"tm": me_tm, "frame": f}

    def at_tm(t):
        return {"tm": t, "frame": me}

    def aligned(n, size):
        return pl.ds(pl.multiple_of(n, size), size)

    def in_part(s):
        return aligned(peer(s) * piece, piece)

    def in_frame(h, s):
        return aligned(h * part + peer(s) * piece, piece)

    def sub_part(g, s):
        return aligned(peer(s) * piece + g * sub, sub)

    def sub_frame(h, g, s):
        return aligned(h * part + peer(s) * piece + g * sub, sub)

    own_start, far_start = side * part, (1 - side) * part
    edge_row = aligned((part_rows - 1 + side) * width, width)
    halo_row = aligned((part_rows - side) * width, width)
    halo = pl.ds(part, width)

    barrier = pltpu.get_barrier_semaphore()

    def batches(size):
        return [list(range(groups))[g : g + size] for g in range(0, groups, size)]

    def greet(device):
        pl.semaphore_signal(barrier, inc=1, device_id=device, device_id_type=pl.DeviceIdType.MESH)

    for s in others:
        greet(at_frame(peer(s)))
    for s in range(n_frame):
        greet({"tm": partner, "frame": peer(s)})

    @pl.when(has_prev)
    def _():
        greet(at_tm(me_tm - 2))

    def meet():
        pl.semaphore_wait(barrier, 2 * n_frame - 1 + has_next.astype(jnp.int32))

    pairs = [
        (freq_hbm, freq_ref),
        (gain_space_hbm, gain_space_ref),
        (wtime_hbm, wtime_ref),
        (guess_hbm, guess_ref),
        (wconv_hbm, wconv_ref),
        (gain_attention_hbm, gain_attention_ref),
        (noise_hbm, noise_ref),
        (wattn_hbm, wattn_ref),
        (wout_hbm, wout_ref),
        (start_hbm, start_ref),
    ]
    loads = [pltpu.make_async_copy(src, dst, load.at[i]) for i, (src, dst) in enumerate(pairs)]
    for copy in loads:
        copy.start()

    edge = jnp.zeros((width, 3 * channels), bf16)
    taps[0:width, :] = edge
    taps[cells + width : cells + 2 * width, :] = edge
    for g in range(2):
        taps_two[g, aligned(side * (part + width), width), :] = edge

    @pl.when(jnp.logical_not(has_prev))
    def _():
        zin[...] = jnp.zeros_like(zin)

    row = lax.broadcasted_iota(jnp.int32, (n_frame * block, n_frame * block), 0)
    lane = lax.broadcasted_iota(jnp.int32, (n_frame * block, n_frame * block), 1)
    same_cell[...] = jnp.where(row % block == lane % block, 0.0, -jnp.inf)
    head_lane = lax.broadcasted_iota(jnp.int32, (n_frame * block, channels), 1) // HEAD_DIM
    heads_of = jnp.where(
        lax.broadcasted_iota(jnp.int32, (8, channels), 0) == lax.broadcasted_iota(jnp.int32, (8, channels), 1) // HEAD_DIM,
        1.0,
        0.0,
    ).astype(bf16)

    for copy in loads[:3]:
        copy.wait()
    step = jnp.full((8, channels), step_ref[0].astype(f32))
    time_value = step[0:1, :] / 1000.0
    coefficient = (0.5 + time_value) / math.sqrt(n_tm)
    angles = step * freq_ref[...]
    position = lax.broadcasted_iota(jnp.int32, (8, channels), 1)
    encoded = jnp.where(position < channels // 2, jnp.cos(angles), jnp.sin(angles))
    shifted = jnp.dot(encoded, wtime_ref[...], precision=lax.Precision.HIGHEST, preferred_element_type=f32)
    gain_space = gain_space_ref[...] * (1.0 + shifted[0:1, :channels])
    offset = shifted[0:1, channels:]
    for k, value in enumerate((gain_space, offset, coefficient, time_value)):
        params[side, k : k + 1, :] = value

    def inverse_rms(v):
        return lax.rsqrt(jnp.mean(v * v, axis=-1, keepdims=True) + EPS)

    def make_taps(x, gain, shift, put):
        rows = x.shape[0]
        column = lax.broadcasted_iota(jnp.int32, x.shape, 0) % width
        normed = x * inverse_rms(x) * gain + shift
        left = jnp.where(column == 0, 0.0, pltpu.roll(normed, 1, 0))
        right = jnp.where(column == width - 1, 0.0, pltpu.roll(normed, rows - 1, 0))
        for k, value in enumerate((left, normed, right)):
            put(slice(k * channels, (k + 1) * channels), value.astype(bf16))

    def first_taps(i, _):
        at = i * piece

        def put(columns, value):
            taps[pl.ds(pl.multiple_of(at + width, width), piece), columns] = value

        make_taps(guess_ref[aligned(at, piece), :], gain_space, offset, put)
        return 0

    loads[3].wait()
    lax.fori_loop(0, 2 * n_frame, first_taps, 0, unroll=4)
    for copy in loads[4:7]:
        copy.wait()
    gain_attention = gain_attention_ref[...]

    def remote(src, dst, send, recv, device):
        return pltpu.make_async_remote_copy(
            src_ref=src,
            dst_ref=dst,
            send_sem=send,
            recv_sem=recv,
            device_id=device,
            device_id_type=pl.DeviceIdType.MESH,
        )

    def x_copy(g, s):
        return remote(
            msend.at[sub_frame(1 - side, g, s)], xin.at[sub_part(g, s)], x_send.at[g, s], x_recv.at[g, s], at_tm(partner)
        )

    def x_halo():
        return remote(msend.at[edge_row], xin.at[halo], x_send.at[0, n_frame], x_recv.at[0, n_frame], at_tm(partner))

    behind_owner, edge_owner = side * last_slot, (1 - side) * last_slot

    def behind_copy(s):
        return remote(hsend.at[0, s], hin.at[0], h_send.at[0, s], h_recv.at[0], at_frame(sender(s)))

    def edge_copy(s):
        return remote(
            hsend.at[1, s], hin.at[1], h_send.at[1, s], h_recv.at[1], {"tm": partner, "frame": sender(s)}
        )

    def cut_row(k, s, behind):
        rows = jnp.concatenate([aout[0, g, s, k * sub : (k + 1) * sub, :] for g in range(groups)], axis=0)
        return jnp.where(behind == 0, rows[:width], rows[piece - width :])

    def noise_copy():
        return remote(
            nsend, noises.at[side], m_send.at[0], m_recv.at[0], at_tm(partner)
        )

    def noise_arrival():
        return remote(
            nsend, noises.at[1 - side], m_send.at[0], m_recv.at[0], at_tm(partner)
        )

    def params_copy(to):
        return remote(params.at[side], params.at[to], m_send.at[1], m_recv.at[1], at_tm(partner))

    def f_copy(g, s):
        return remote(
            fsend.at[sub_part(g, s)], fin.at[sub_part(g, s)], f_send.at[g, s], f_recv.at[g, s], at_tm(partner)
        )

    def z_copy(turn, g, s, rows):
        return remote(
            zout.at[turn, rows], zin.at[turn, rows], z_send.at[turn, g, s], z_recv.at[turn, g, s], at_tm(me_tm + 2)
        )

    for turn in range(ITERS):
        last = turn == ITERS - 1

        def in_copy(s, g):
            return remote(
                ain.at[turn, g, s], rin.at[turn, g, s], in_send.at[turn, g, s], in_recv.at[turn, g, s], at_frame(peer(s))
            )

        def out_copy(s, g):
            rows = pl.ds(sub, sub) if turn == 0 else pl.ds(0, unit)
            return remote(
                aout.at[turn, g, s, rows],
                rout.at[turn, g, s, rows],
                out_send.at[turn, g, s],
                out_recv.at[turn, g, s],
                at_frame(sender(s)),
            )

        def over_copy(s, g):
            return remote(
                aout.at[0, g, s, pl.ds(0, sub)],
                rout.at[0, g, s, pl.ds(0, sub)],
                o_send.at[g, s],
                o_recv.at[g, s],
                {"tm": partner, "frame": sender(s)},
            )

        def frame_part(k):
            return 1 - side if k == 0 else side

        def near_rows(k, g, s, r):
            at = peer(s) * piece + g * sub + r * width
            if turn == 0:
                return taps[pl.ds(pl.multiple_of(frame_part(k) * part + at, 16), sub), :]
            return taps_two[k, pl.ds(pl.multiple_of(at, 16), sub), :]

        def mix(gs, slots):
            each = [(g, s, k) for g in gs for s in slots for k in range(2)]
            near = [jnp.concatenate([near_rows(k, g, s, r) for r in range(3)], axis=1) for g, s, k in each]
            total = jnp.dot(jnp.concatenate(near, axis=0), wconv_ref[...], preferred_element_type=f32)
            if turn == 0:
                here = [guess_ref[sub_frame(frame_part(k), g, s), :] for g, s, k in each]
            else:
                here = [states[k, sub_part(g, s), :] for g, s, k in each]
            value = jnp.concatenate(here, axis=0) + total * (0.5 + 0.5 * jnp.tanh(0.5 * total))
            normed = (value * inverse_rms(value) * gain_attention).astype(bf16)
            for i, (g, s) in enumerate((g, s) for g in gs for s in slots):
                ain[turn, g, s] = normed[i * unit : (i + 1) * unit]
                if s != last_slot:
                    in_copy(s, g).start()
            for i, (g, s, k) in enumerate(each):
                mine = value[i * sub : (i + 1) * sub]
                if turn == 0:
                    rows = sub_frame(frame_part(k), g, s)
                    known = coefficient * (mine + time_value * noise_ref[rows, :])
                    term[rows, :] = known
                    msend[rows, :] = known.astype(bf16)
                    if k == 0:
                        x_copy(g, s).start()
                else:
                    noise = noises[k, sub_part(g, s), :].astype(f32)
                    base[g, s, k * sub : (k + 1) * sub] = params[k, 2:3, :] * (mine + params[k, 3:4, :] * noise)

        def project(g, blocks, slots):
            result = jnp.dot(jnp.concatenate(blocks, axis=0), wattn_ref[...], preferred_element_type=f32).astype(bf16)
            for k, s in enumerate(slots):
                proj[g, s] = result[k * unit : (k + 1) * unit]

        def attend(g):
            for b in range(unit // block):
                rows = slice(b * block, (b + 1) * block)
                query, key, value = (
                    jnp.concatenate([proj[g, s, rows, k * channels : (k + 1) * channels] for s in range(n_frame)], axis=0)
                    for k in range(3)
                )
                by_head = jnp.concatenate([query * heads_of[h : h + 1, :] for h in range(heads)], axis=0)
                scores = lax.dot_general(by_head, key, (((1,), (1,)), ((), ())), preferred_element_type=f32)
                scores = scores * (1.0 / math.sqrt(HEAD_DIM)) + jnp.concatenate([same_cell[...]] * heads, axis=0)
                raised = jnp.exp(scores - jnp.max(scores, axis=-1, keepdims=True))
                weights = (raised * (1.0 / jnp.sum(raised, axis=-1, keepdims=True))).astype(bf16)
                result = jnp.dot(weights, value, preferred_element_type=f32)
                size = n_frame * block
                mixed_heads = result[:size]
                for h in range(1, heads):
                    mixed_heads = jnp.where(head_lane == h, result[h * size : (h + 1) * size], mixed_heads)
                for s in range(n_frame):
                    aout[turn, g, s, rows, :] = mixed_heads[s * block : (s + 1) * block].astype(bf16)
            for s in range(n_frame):
                if turn == 0:
                    over_copy(s, g).start()
                if s != last_slot:
                    out_copy(s, g).start()

        def close(g, blocks, slots):
            result = jnp.dot(jnp.concatenate(blocks, axis=0), wout_ref[...], preferred_element_type=f32)
            for i, s in enumerate(slots):
                first, second = result[i * unit : i * unit + sub], result[i * unit + sub : (i + 1) * unit]
                if turn == 0:
                    other[sub_part(g, s), :] = xin[sub_part(g, s), :].astype(f32) + params[1 - side, 2:3, :] * first
                    term[sub_frame(side, g, s), :] += coefficient * second
                else:
                    base[g, s, 0:sub] += params[0, 2:3, :] * first
                    base[g, s, sub:unit] += params[1, 2:3, :] * second

        def settle(g, slots):
            sums = []
            for s in slots:
                rows = sub_part(g, s)

                @pl.when(has_prev)
                def _():
                    z_copy(turn, g, s, rows).wait_recv()

                first = zin[turn, rows, :].astype(f32) + base[g, s, 0:sub]
                second = first + base[g, s, sub:unit]
                zout[turn, rows, :] = second.astype(bf16)

                @pl.when(has_next)
                def _():
                    z_copy(turn, g, s, rows).start()

                fsend[rows, :] = jnp.where(side == 0, second, first).astype(bf16)
                f_copy(g, s).start()
                sums.append(jnp.where(side == 0, first, second))
            for s, value in zip(slots, sums, strict=True):
                mine = sub_frame(side, g, s)
                out_ref[mine, :] = start_ref[mine, :] + value

        def chain(g, s, rows, nat):
            @pl.when(has_prev)
            def _():
                z_copy(turn, g, s, rows).wait_recv()

            total = zin[turn, rows, :].astype(f32) + (term[nat, :] + other[rows, :])
            zout[turn, rows, :] = total.astype(bf16)
            z_copy(turn, g, s, rows).start()

        if turn == 0:
            meet()
        for gs in batches(1):
            mix(gs, far_slots)
        if turn == 0:
            nsend[...] = noise_ref[aligned(far_start, part), :].astype(bf16)
            noise_copy().start()
        for gs in batches(1):
            mix(gs, near_slots)
        if turn == 0:
            x_halo().start()
            params_copy(side).start()
            for copy in loads[7:]:
                copy.wait()
            noises[side] = noise_ref[aligned(own_start, part), :].astype(bf16)
        for g in range(groups):
            project(g, [ain[turn, g, last_slot]], [last_slot])
        for g in range(groups):
            for s in reversed(others):
                in_copy(s, g).wait_recv()
            project(g, [rin[turn, g, s] for s in others], others)
            attend(g)
        if turn == 0:

            @pl.when(me == behind_owner)
            def _():
                for s in others:
                    hsend[0, s] = cut_row(0, s, side)
                    behind_copy(s).start()
                hin[0] = cut_row(0, last_slot, side)

            @pl.when(me == edge_owner)
            def _():
                for s in range(n_frame):
                    hsend[1, s] = cut_row(1, s, 1 - side)
                    edge_copy(s).start()

            params_copy(1 - side).wait_recv()
        for g in range(groups):
            for s in others:
                in_copy(s, g).wait_send()
        for g in range(groups):
            if turn == 0:
                for s in range(n_frame):
                    x_copy(g, s).wait_recv()
                for s in reversed(range(n_frame)):
                    over_copy(s, g).wait_recv()
            else:
                close(g, [aout[turn, g, last_slot]], [last_slot])
                settle(g, [last_slot])
            for s in reversed(others):
                out_copy(s, g).wait_recv()
            if turn == 0:
                mine = jnp.concatenate([rout[0, g, last_slot, 0:sub, :], aout[0, g, last_slot, sub:unit, :]], axis=0)
                close(g, [rout[0, g, s] for s in others] + [mine], others + [last_slot])

                @pl.when(has_next)
                def _():
                    for s in range(n_frame):
                        chain(g, s, sub_part(g, s), sub_frame(side, g, s))

            else:
                close(g, [rout[turn, g, s] for s in others], others)
                settle(g, others)
        if turn == 0:

            @pl.when(me != behind_owner)
            def _():
                behind_copy(0).wait_recv()

            edge_copy(0).wait_recv()
            x_halo().wait_recv()
            beside = jnp.concatenate([hin[0], hin[1]], axis=0)
            result = jnp.dot(beside, wout_ref[...], preferred_element_type=f32)
            term[halo_row, :] += coefficient * result[:width]
            other[halo, :] = xin[halo, :].astype(f32) + params[1 - side, 2:3, :] * result[width:]

        if not last:

            @pl.when(has_next)
            def _():
                chain(0, n_frame, halo, halo_row)

            for g in range(groups):
                for s in range(n_frame):
                    over_copy(s, g).wait_send()
                    if s != last_slot:
                        out_copy(s, g).wait_send()

            @pl.when(me == behind_owner)
            def _():
                for s in others:
                    behind_copy(s).wait_send()

            @pl.when(me == edge_owner)
            def _():
                for s in range(n_frame):
                    edge_copy(s).wait_send()

            noise_arrival().wait_recv()
            noise_copy().wait_send()
            params_copy(side).wait_send()

            def begin(rows, nat, at, keep):
                first = start_ref[nat, :] + zin[turn, rows, :].astype(f32)
                second = first + jnp.where(side == 0, term[nat, :], other[rows, :])
                for g, x in enumerate((first, second)):
                    if keep:
                        states[g, rows, :] = x

                    def put(columns, value):
                        taps_two[g, pl.ds(pl.multiple_of(at, width), x.shape[0]), columns] = value

                    make_taps(x, params[g, 0:1, :], params[g, 1:2, :], put)

            end_of_chain = jnp.logical_and(jnp.logical_not(has_next), has_prev)

            def begin_slot(s, _):
                @pl.when(end_of_chain)
                def _():
                    for g in range(groups):
                        z_copy(turn, g, s, sub_part(g, s)).wait_recv()

                begin(in_part(s), in_frame(side, s), peer(s) * piece + width, True)
                return 0

            lax.fori_loop(0, n_frame, begin_slot, 0, unroll=True)

            @pl.when(end_of_chain)
            def _():
                z_copy(turn, 0, n_frame, halo).wait_recv()

            begin(halo, halo_row, (1 - side) * (part + width), False)

            def sent(s, _):
                for g in range(groups):
                    x_copy(g, s).wait_send()

                    @pl.when(has_next)
                    def _():
                        z_copy(turn, g, s, sub_part(g, s)).wait_send()

                return 0

            lax.fori_loop(0, n_frame, sent, 0)
            x_halo().wait_send()

            @pl.when(has_next)
            def _():
                z_copy(turn, 0, n_frame, halo).wait_send()

    def receive(i, _):
        g, s = lax.div(i, n_frame), lax.rem(i, n_frame)
        f_copy(g, s).wait_recv()
        rows = sub_frame(1 - side, g, s)
        out_ref[rows, :] = start_ref[rows, :] + fin[sub_part(g, s), :].astype(f32)
        return 0


    def sent_last(i, _):
        g, s = lax.div(i, n_frame), lax.rem(i, n_frame)
        z_copy(ITERS - 1, g, s, sub_part(g, s)).wait_send()
        return 0

    def sent_over(i, _):
        f_copy(lax.div(i, n_frame), lax.rem(i, n_frame)).wait_send()
        return 0

    for g in range(groups):
        for s in others:
            remote(
                aout.at[ITERS - 1, g, s],
                rout.at[ITERS - 1, g, s],
                out_send.at[ITERS - 1, g, s],
                out_recv.at[ITERS - 1, g, s],
                at_frame(sender(s)),
            ).wait_send()

    @pl.when(has_next)
    def _():
        lax.fori_loop(0, groups * n_frame, sent_last, 0)

    lax.fori_loop(0, groups * n_frame, receive, 0)
    lax.fori_loop(0, groups * n_frame, sent_over, 0)


def shards(
    n_tm,
    n_frame,
    start_state,
    initial_guess,
    noise_draws,
    timesteps,
    gain_space,
    gain_attention,
    time_weight,
    space_weight,
    attention_weight,
    output_weight,
):
    _, height, width, channels = start_state.shape
    cells = height * width
    part = cells // 2
    piece = part // n_frame
    groups = min(GROUPS, piece // 16)
    block = min(max(16, 128 // n_frame), piece // groups)
    half_width = channels // 2
    frequency = np.exp(-math.log(10000.0) * np.arange(half_width) / half_width).astype(np.float32)
    frequency = np.concatenate([frequency, frequency])[None]
    f32, bf16 = jnp.float32, jnp.bfloat16
    dma, vmem = pltpu.SemaphoreType.DMA, pltpu.VMEM
    field = vmem((cells, channels), f32)
    row = vmem((1, channels), f32)
    exchange = vmem((ITERS, groups, n_frame, 2 * piece // groups, channels), bf16)
    carried = vmem((ITERS, part + width, channels), bf16)
    anywhere = pl.BlockSpec(memory_space=pl.ANY)
    total = pl.pallas_call(
        functools.partial(kernel, n_tm, n_frame, width, groups),
        out_shape=pltpu.VMEM((cells, channels), f32),
        in_specs=[pl.BlockSpec(memory_space=pltpu.SMEM)] + [anywhere] * 10,
        out_specs=pl.BlockSpec(memory_space=pltpu.VMEM),
        scratch_shapes=[
            field,
            field,
            field,
            row,
            row,
            row,
            vmem(time_weight.shape, f32),
            vmem(space_weight.shape, bf16),
            vmem(attention_weight.shape, bf16),
            vmem(output_weight.shape, bf16),
            vmem((n_frame * block, n_frame * block), f32),
            vmem((2, 8, channels), f32),
            vmem((2, part, channels), bf16),
            vmem((2, part, channels), f32),
            vmem((cells + 2 * width, 3 * channels), bf16),
            vmem((2, part + 2 * width, 3 * channels), bf16),
            vmem((groups, n_frame, 2 * piece // groups, channels), f32),
            field,
            vmem((groups, n_frame, 2 * piece // groups, 3 * channels), bf16),
            exchange,
            exchange,
            exchange,
            exchange,
            vmem((cells, channels), bf16),
            vmem((part + width, channels), bf16),
            vmem((part + width, channels), f32),
            vmem((part, channels), bf16),
            vmem((2, n_frame, width, channels), bf16),
            vmem((2, width, channels), bf16),
            carried,
            carried,
            vmem((part, channels), bf16),
            vmem((part, channels), bf16),
            dma((10,)),
            *([dma((ITERS, groups, n_frame))] * 4),
            *([dma((groups, n_frame + 1))] * 2),
            *([dma((ITERS, groups, n_frame + 1))] * 2),
            *([dma((groups, n_frame))] * 2),
            *([dma((2,))] * 2),
            dma((2, n_frame)),
            dma((2,)),
            *([dma((groups, n_frame))] * 2),
        ],
        compiler_params=pltpu.CompilerParams(collective_id=0, has_side_effects=True),
    )(
        timesteps,
        start_state.reshape(cells, channels),
        initial_guess.reshape(cells, channels),
        noise_draws.reshape(cells, channels),
        jnp.asarray(frequency),
        gain_space[None],
        gain_attention[None],
        time_weight,
        space_weight,
        attention_weight,
        output_weight,
    )
    return total.reshape(1, 1, height, width, channels)


def solution(mesh):
    return jax.shard_map(
        functools.partial(shards, mesh.shape["tm"], mesh.shape["frame"]),
        mesh=mesh,
        in_specs=(
            P("frame", None, None, None),
            P("tm", "frame", None, None, None),
            P("tm", "frame", None, None, None),
            P("tm"),
            P(),
            P(),
            P(),
            P(),
            P(),
            P(),
        ),
        out_specs=P("tm", "frame", None, None, None),
        check_vma=False,
    )
```

```python
import functools
import math

import jax
import jax.numpy as jnp
import numpy as np
from jax import lax
from jax.experimental import pallas as pl
from jax.experimental.pallas import tpu as pltpu
from jax.sharding import PartitionSpec as P

HEAD_DIM = 64
ITERS = 2
GROUPS = 2
EPS = 1e-06


def kernel(
    n_tm,
    n_frame,
    width,
    groups,
    step_ref,
    start_hbm,
    guess_hbm,
    noise_hbm,
    freq_hbm,
    gain_space_hbm,
    gain_attention_hbm,
    wtime_hbm,
    wconv_hbm,
    wattn_hbm,
    wout_hbm,
    out_ref,
    start_ref,
    guess_ref,
    noise_ref,
    freq_ref,
    gain_space_ref,
    gain_attention_ref,
    wtime_ref,
    wconv_ref,
    wattn_ref,
    wout_ref,
    same_cell,
    params,
    noises,
    states,
    taps,
    taps_two,
    base,
    term,
    proj,
    ain,
    rin,
    aout,
    rout,
    msend,
    xin,
    other,
    nsend,
    hsend,
    hin,
    zin,
    zout,
    fsend,
    fin,
    load,
    in_send,
    in_recv,
    out_send,
    out_recv,
    x_send,
    x_recv,
    z_send,
    z_recv,
    f_send,
    f_recv,
    m_send,
    m_recv,
    h_send,
    h_recv,
    o_send,
    o_recv,
):
    cells, channels = start_hbm.shape
    part = cells // 2
    piece = part // n_frame
    part_rows = part // width
    sub = piece // groups
    unit = 2 * sub
    chips = n_frame // 2
    heads = channels // HEAD_DIM
    block = min(max(16, 128 // n_frame), piece // groups)
    f32, bf16 = jnp.float32, jnp.bfloat16
    me_tm = lax.axis_index("tm")
    me = lax.axis_index("frame")
    my_chip, my_core = me // 2, lax.rem(me, 2)
    link, side = me_tm // 2, lax.rem(me_tm, 2)
    links = n_tm // 2
    has_prev = link > 0
    has_next = link < links - 1
    partner = me_tm + 1 - 2 * side

    last_slot = n_frame - 1
    far_slots = list(range(n_frame - 2))
    near_slots = [n_frame - 2, last_slot]
    others = list(range(last_slot))

    def peer(s):
        chip = lax.rem(my_chip + 1 + lax.div(s, 2), chips)
        return 2 * chip + lax.rem(my_core + s + lax.div(s + 2, n_frame), 2)

    def sender(s):
        chip = lax.rem(my_chip + 2 * chips - 1 - lax.div(s, 2), chips)
        return 2 * chip + lax.rem(my_core + s + lax.div(s + 2, n_frame), 2)

    def at_frame(f):
        return {"tm": me_tm, "frame": f}

    def at_tm(t):
        return {"tm": t, "frame": me}

    def aligned(n, size):
        return pl.ds(pl.multiple_of(n, size), size)

    def in_part(s):
        return aligned(peer(s) * piece, piece)

    def in_frame(h, s):
        return aligned(h * part + peer(s) * piece, piece)

    def sub_part(g, s):
        return aligned(peer(s) * piece + g * sub, sub)

    def sub_frame(h, g, s):
        return aligned(h * part + peer(s) * piece + g * sub, sub)

    own_start, far_start = side * part, (1 - side) * part
    edge_row = aligned((part_rows - 1 + side) * width, width)
    halo_row = aligned((part_rows - side) * width, width)
    halo = pl.ds(part, width)

    barrier = pltpu.get_barrier_semaphore()

    def batches(size):
        return [list(range(groups))[g : g + size] for g in range(0, groups, size)]

    def greet(device):
        pl.semaphore_signal(barrier, inc=1, device_id=device, device_id_type=pl.DeviceIdType.MESH)

    for s in others:
        greet(at_frame(peer(s)))
    for s in range(n_frame):
        greet({"tm": partner, "frame": peer(s)})

    @pl.when(has_prev)
    def _():
        greet(at_tm(me_tm - 2))

    def meet():
        pl.semaphore_wait(barrier, 2 * n_frame - 1 + has_next.astype(jnp.int32))

    pairs = [
        (freq_hbm, freq_ref),
        (gain_space_hbm, gain_space_ref),
        (wtime_hbm, wtime_ref),
        (guess_hbm.at[pl.ds(0, part)], guess_ref.at[pl.ds(0, part)]),
        (guess_hbm.at[pl.ds(part, part)], guess_ref.at[pl.ds(part, part)]),
        (wconv_hbm, wconv_ref),
        (gain_attention_hbm, gain_attention_ref),
        (noise_hbm, noise_ref),
        (wattn_hbm, wattn_ref),
        (wout_hbm, wout_ref),
        (start_hbm, start_ref),
    ]
    loads = [pltpu.make_async_copy(src, dst, load.at[i]) for i, (src, dst) in enumerate(pairs)]
    for copy in loads:
        copy.start()

    edge = jnp.zeros((width, 3 * channels), bf16)
    taps[0:width, :] = edge
    taps[cells + width : cells + 2 * width, :] = edge
    for g in range(2):
        taps_two[g, aligned(side * (part + width), width), :] = edge

    @pl.when(jnp.logical_not(has_prev))
    def _():
        zin[...] = jnp.zeros_like(zin)

    row = lax.broadcasted_iota(jnp.int32, (n_frame * block, n_frame * block), 0)
    lane = lax.broadcasted_iota(jnp.int32, (n_frame * block, n_frame * block), 1)
    same_cell[...] = jnp.where(row % block == lane % block, 0.0, -jnp.inf)
    head_lane = lax.broadcasted_iota(jnp.int32, (n_frame * block, channels), 1) // HEAD_DIM
    heads_of = jnp.where(
        lax.broadcasted_iota(jnp.int32, (8, channels), 0) == lax.broadcasted_iota(jnp.int32, (8, channels), 1) // HEAD_DIM,
        1.0,
        0.0,
    ).astype(bf16)

    loads[0].wait()
    step = jnp.full((8, channels), step_ref[0].astype(f32))
    time_value = step[0:1, :] / 1000.0
    coefficient = (0.5 + time_value) / math.sqrt(n_tm)
    angles = step * freq_ref[...]
    position = lax.broadcasted_iota(jnp.int32, (8, channels), 1)
    encoded = jnp.where(position < channels // 2, jnp.cos(angles), jnp.sin(angles))
    for copy in loads[1:3]:
        copy.wait()
    shifted = jnp.dot(encoded, wtime_ref[...], precision=lax.Precision.HIGHEST, preferred_element_type=f32)
    gain_space = gain_space_ref[...] * (1.0 + shifted[0:1, :channels])
    offset = shifted[0:1, channels:]
    for k, value in enumerate((gain_space, offset, coefficient, time_value)):
        params[side, k : k + 1, :] = value

    def inverse_rms(v):
        return lax.rsqrt(jnp.mean(v * v, axis=-1, keepdims=True) + EPS)

    def make_taps(x, gain, shift, put):
        rows = x.shape[0]
        column = lax.broadcasted_iota(jnp.int32, x.shape, 0) % width
        normed = x * inverse_rms(x) * gain + shift
        left = jnp.where(column == 0, 0.0, pltpu.roll(normed, 1, 0))
        right = jnp.where(column == width - 1, 0.0, pltpu.roll(normed, rows - 1, 0))
        for k, value in enumerate((left, normed, right)):
            put(slice(k * channels, (k + 1) * channels), value.astype(bf16))

    def first_taps(i, _):
        at = i * piece

        def put(columns, value):
            taps[pl.ds(pl.multiple_of(at + width, width), piece), columns] = value

        make_taps(guess_ref[aligned(at, piece), :], gain_space, offset, put)
        return 0

    loads[3].wait()
    lax.fori_loop(0, n_frame, first_taps, 0, unroll=4)
    loads[4].wait()
    lax.fori_loop(n_frame, 2 * n_frame, first_taps, 0, unroll=4)
    for copy in loads[5:8]:
        copy.wait()
    gain_attention = gain_attention_ref[...]

    def remote(src, dst, send, recv, device):
        return pltpu.make_async_remote_copy(
            src_ref=src,
            dst_ref=dst,
            send_sem=send,
            recv_sem=recv,
            device_id=device,
            device_id_type=pl.DeviceIdType.MESH,
        )

    def x_copy(g, s):
        return remote(
            msend.at[sub_frame(1 - side, g, s)], xin.at[sub_part(g, s)], x_send.at[g, s], x_recv.at[g, s], at_tm(partner)
        )

    def x_halo():
        return remote(msend.at[edge_row], xin.at[halo], x_send.at[0, n_frame], x_recv.at[0, n_frame], at_tm(partner))

    behind_owner, edge_owner = side * last_slot, (1 - side) * last_slot

    def behind_copy(s):
        return remote(hsend.at[0, s], hin.at[0], h_send.at[0, s], h_recv.at[0], at_frame(sender(s)))

    def edge_copy(s):
        return remote(
            hsend.at[1, s], hin.at[1], h_send.at[1, s], h_recv.at[1], {"tm": partner, "frame": sender(s)}
        )

    def cut_row(k, s, behind):
        rows = jnp.concatenate([aout[0, g, s, k * sub : (k + 1) * sub, :] for g in range(groups)], axis=0)
        return jnp.where(behind == 0, rows[:width], rows[piece - width :])

    def noise_copy():
        return remote(
            nsend, noises.at[side], m_send.at[0], m_recv.at[0], at_tm(partner)
        )

    def noise_arrival():
        return remote(
            nsend, noises.at[1 - side], m_send.at[0], m_recv.at[0], at_tm(partner)
        )

    def params_copy(to):
        return remote(params.at[side], params.at[to], m_send.at[1], m_recv.at[1], at_tm(partner))

    def f_copy(g, s):
        return remote(
            fsend.at[sub_part(g, s)], fin.at[sub_part(g, s)], f_send.at[g, s], f_recv.at[g, s], at_tm(partner)
        )

    def z_copy(turn, g, s, rows):
        return remote(
            zout.at[turn, rows], zin.at[turn, rows], z_send.at[turn, g, s], z_recv.at[turn, g, s], at_tm(me_tm + 2)
        )

    for turn in range(ITERS):
        last = turn == ITERS - 1

        def in_copy(s, g):
            return remote(
                ain.at[turn, g, s], rin.at[turn, g, s], in_send.at[turn, g, s], in_recv.at[turn, g, s], at_frame(peer(s))
            )

        def out_copy(s, g):
            rows = pl.ds(sub, sub) if turn == 0 else pl.ds(0, unit)
            return remote(
                aout.at[turn, g, s, rows],
                rout.at[turn, g, s, rows],
                out_send.at[turn, g, s],
                out_recv.at[turn, g, s],
                at_frame(sender(s)),
            )

        def over_copy(s, g):
            return remote(
                aout.at[0, g, s, pl.ds(0, sub)],
                rout.at[0, g, s, pl.ds(0, sub)],
                o_send.at[g, s],
                o_recv.at[g, s],
                {"tm": partner, "frame": sender(s)},
            )

        def frame_part(k):
            return 1 - side if k == 0 else side

        def near_rows(k, g, s, r):
            at = peer(s) * piece + g * sub + r * width
            if turn == 0:
                return taps[pl.ds(pl.multiple_of(frame_part(k) * part + at, 16), sub), :]
            return taps_two[k, pl.ds(pl.multiple_of(at, 16), sub), :]

        def mix(gs, slots):
            each = [(g, s, k) for g in gs for s in slots for k in range(2)]
            near = [jnp.concatenate([near_rows(k, g, s, r) for r in range(3)], axis=1) for g, s, k in each]
            total = jnp.dot(jnp.concatenate(near, axis=0), wconv_ref[...], preferred_element_type=f32)
            if turn == 0:
                here = [guess_ref[sub_frame(frame_part(k), g, s), :] for g, s, k in each]
            else:
                here = [states[k, sub_part(g, s), :] for g, s, k in each]
            value = jnp.concatenate(here, axis=0) + total * (0.5 + 0.5 * jnp.tanh(0.5 * total))
            normed = (value * inverse_rms(value) * gain_attention).astype(bf16)
            for i, (g, s) in enumerate((g, s) for g in gs for s in slots):
                ain[turn, g, s] = normed[i * unit : (i + 1) * unit]
                if s != last_slot:
                    in_copy(s, g).start()
            for i, (g, s, k) in enumerate(each):
                mine = value[i * sub : (i + 1) * sub]
                if turn == 0:
                    rows = sub_frame(frame_part(k), g, s)
                    known = coefficient * (mine + time_value * noise_ref[rows, :])
                    term[rows, :] = known
                    msend[rows, :] = known.astype(bf16)
                    if k == 0:
                        x_copy(g, s).start()
                else:
                    noise = noises[k, sub_part(g, s), :].astype(f32)
                    base[g, s, k * sub : (k + 1) * sub] = params[k, 2:3, :] * (mine + params[k, 3:4, :] * noise)

        def project(g, blocks, slots):
            result = jnp.dot(jnp.concatenate(blocks, axis=0), wattn_ref[...], preferred_element_type=f32).astype(bf16)
            for k, s in enumerate(slots):
                proj[g, s] = result[k * unit : (k + 1) * unit]

        def attend(g):
            for b in range(unit // block):
                rows = slice(b * block, (b + 1) * block)
                query, key, value = (
                    jnp.concatenate([proj[g, s, rows, k * channels : (k + 1) * channels] for s in range(n_frame)], axis=0)
                    for k in range(3)
                )
                by_head = jnp.concatenate([query * heads_of[h : h + 1, :] for h in range(heads)], axis=0)
                scores = lax.dot_general(by_head, key, (((1,), (1,)), ((), ())), preferred_element_type=f32)
                scores = scores * (1.0 / math.sqrt(HEAD_DIM)) + jnp.concatenate([same_cell[...]] * heads, axis=0)
                raised = jnp.exp(scores - jnp.max(scores, axis=-1, keepdims=True))
                weights = (raised * (1.0 / jnp.sum(raised, axis=-1, keepdims=True))).astype(bf16)
                result = jnp.dot(weights, value, preferred_element_type=f32)
                size = n_frame * block
                mixed_heads = result[:size]
                for h in range(1, heads):
                    mixed_heads = jnp.where(head_lane == h, result[h * size : (h + 1) * size], mixed_heads)
                for s in range(n_frame):
                    aout[turn, g, s, rows, :] = mixed_heads[s * block : (s + 1) * block].astype(bf16)
            for s in range(n_frame):
                if turn == 0:
                    over_copy(s, g).start()
                if s != last_slot:
                    out_copy(s, g).start()

        def close(g, blocks, slots):
            result = jnp.dot(jnp.concatenate(blocks, axis=0), wout_ref[...], preferred_element_type=f32)
            for i, s in enumerate(slots):
                first, second = result[i * unit : i * unit + sub], result[i * unit + sub : (i + 1) * unit]
                if turn == 0:
                    other[sub_part(g, s), :] = xin[sub_part(g, s), :].astype(f32) + params[1 - side, 2:3, :] * first
                    term[sub_frame(side, g, s), :] += coefficient * second
                else:
                    base[g, s, 0:sub] += params[0, 2:3, :] * first
                    base[g, s, sub:unit] += params[1, 2:3, :] * second

        def settle(g, slots):
            sums = []
            for s in slots:
                rows = sub_part(g, s)

                @pl.when(has_prev)
                def _():
                    z_copy(turn, g, s, rows).wait_recv()

                first = zin[turn, rows, :].astype(f32) + base[g, s, 0:sub]
                second = first + base[g, s, sub:unit]
                zout[turn, rows, :] = second.astype(bf16)

                @pl.when(has_next)
                def _():
                    z_copy(turn, g, s, rows).start()

                fsend[rows, :] = jnp.where(side == 0, second, first).astype(bf16)
                f_copy(g, s).start()
                sums.append(jnp.where(side == 0, first, second))
            for s, value in zip(slots, sums, strict=True):
                mine = sub_frame(side, g, s)
                out_ref[mine, :] = start_ref[mine, :] + value

        def chain(g, s, rows, nat):
            @pl.when(has_prev)
            def _():
                z_copy(turn, g, s, rows).wait_recv()

            total = zin[turn, rows, :].astype(f32) + (term[nat, :] + other[rows, :])
            zout[turn, rows, :] = total.astype(bf16)
            z_copy(turn, g, s, rows).start()

        if turn == 0:
            meet()
        for gs in batches(1):
            mix(gs, far_slots)
        if turn == 0:
            nsend[...] = noise_ref[aligned(far_start, part), :].astype(bf16)
            noise_copy().start()
        for gs in batches(1):
            mix(gs, near_slots)
        if turn == 0:
            x_halo().start()
            params_copy(side).start()
            for copy in loads[8:]:
                copy.wait()
            noises[side] = noise_ref[aligned(own_start, part), :].astype(bf16)
        for g in range(groups):
            project(g, [ain[turn, g, last_slot]], [last_slot])
        for g in range(groups):
            for s in reversed(others):
                in_copy(s, g).wait_recv()
            project(g, [rin[turn, g, s] for s in others], others)
            attend(g)
        if turn == 0:

            @pl.when(me == behind_owner)
            def _():
                for s in others:
                    hsend[0, s] = cut_row(0, s, side)
                    behind_copy(s).start()
                hin[0] = cut_row(0, last_slot, side)

            @pl.when(me == edge_owner)
            def _():
                for s in range(n_frame):
                    hsend[1, s] = cut_row(1, s, 1 - side)
                    edge_copy(s).start()

            params_copy(1 - side).wait_recv()
        for g in range(groups):
            for s in others:
                in_copy(s, g).wait_send()
        for g in range(groups):
            if turn == 0:
                for s in range(n_frame):
                    x_copy(g, s).wait_recv()
                for s in reversed(range(n_frame)):
                    over_copy(s, g).wait_recv()
            else:
                close(g, [aout[turn, g, last_slot]], [last_slot])
                settle(g, [last_slot])
            for s in reversed(others):
                out_copy(s, g).wait_recv()
            if turn == 0:
                mine = jnp.concatenate([rout[0, g, last_slot, 0:sub, :], aout[0, g, last_slot, sub:unit, :]], axis=0)
                close(g, [rout[0, g, s] for s in others] + [mine], others + [last_slot])

                @pl.when(has_next)
                def _():
                    for s in range(n_frame):
                        chain(g, s, sub_part(g, s), sub_frame(side, g, s))

            else:
                close(g, [rout[turn, g, s] for s in others], others)
                settle(g, others)
        if turn == 0:

            @pl.when(me != behind_owner)
            def _():
                behind_copy(0).wait_recv()

            edge_copy(0).wait_recv()
            x_halo().wait_recv()
            beside = jnp.concatenate([hin[0], hin[1]], axis=0)
            result = jnp.dot(beside, wout_ref[...], preferred_element_type=f32)
            term[halo_row, :] += coefficient * result[:width]
            other[halo, :] = xin[halo, :].astype(f32) + params[1 - side, 2:3, :] * result[width:]

        if not last:

            @pl.when(has_next)
            def _():
                chain(0, n_frame, halo, halo_row)

            for g in range(groups):
                for s in range(n_frame):
                    over_copy(s, g).wait_send()
                    if s != last_slot:
                        out_copy(s, g).wait_send()

            @pl.when(me == behind_owner)
            def _():
                for s in others:
                    behind_copy(s).wait_send()

            @pl.when(me == edge_owner)
            def _():
                for s in range(n_frame):
                    edge_copy(s).wait_send()

            noise_arrival().wait_recv()
            noise_copy().wait_send()
            params_copy(side).wait_send()

            def begin(rows, nat, at, keep):
                first = start_ref[nat, :] + zin[turn, rows, :].astype(f32)
                second = first + jnp.where(side == 0, term[nat, :], other[rows, :])
                for g, x in enumerate((first, second)):
                    if keep:
                        states[g, rows, :] = x

                    def put(columns, value):
                        taps_two[g, pl.ds(pl.multiple_of(at, width), x.shape[0]), columns] = value

                    make_taps(x, params[g, 0:1, :], params[g, 1:2, :], put)

            end_of_chain = jnp.logical_and(jnp.logical_not(has_next), has_prev)

            def begin_slot(s, _):
                @pl.when(end_of_chain)
                def _():
                    for g in range(groups):
                        z_copy(turn, g, s, sub_part(g, s)).wait_recv()

                begin(in_part(s), in_frame(side, s), peer(s) * piece + width, True)
                return 0

            lax.fori_loop(0, n_frame, begin_slot, 0, unroll=True)

            @pl.when(end_of_chain)
            def _():
                z_copy(turn, 0, n_frame, halo).wait_recv()

            begin(halo, halo_row, (1 - side) * (part + width), False)

            def sent(s, _):
                for g in range(groups):
                    x_copy(g, s).wait_send()

                    @pl.when(has_next)
                    def _():
                        z_copy(turn, g, s, sub_part(g, s)).wait_send()

                return 0

            lax.fori_loop(0, n_frame, sent, 0)
            x_halo().wait_send()

            @pl.when(has_next)
            def _():
                z_copy(turn, 0, n_frame, halo).wait_send()

    def receive(i, _):
        g, s = lax.div(i, n_frame), lax.rem(i, n_frame)
        f_copy(g, s).wait_recv()
        rows = sub_frame(1 - side, g, s)
        out_ref[rows, :] = start_ref[rows, :] + fin[sub_part(g, s), :].astype(f32)
        return 0


    def sent_last(i, _):
        g, s = lax.div(i, n_frame), lax.rem(i, n_frame)
        z_copy(ITERS - 1, g, s, sub_part(g, s)).wait_send()
        return 0

    def sent_over(i, _):
        f_copy(lax.div(i, n_frame), lax.rem(i, n_frame)).wait_send()
        return 0

    for g in range(groups):
        for s in others:
            remote(
                aout.at[ITERS - 1, g, s],
                rout.at[ITERS - 1, g, s],
                out_send.at[ITERS - 1, g, s],
                out_recv.at[ITERS - 1, g, s],
                at_frame(sender(s)),
            ).wait_send()

    @pl.when(has_next)
    def _():
        lax.fori_loop(0, groups * n_frame, sent_last, 0)

    lax.fori_loop(0, groups * n_frame, receive, 0)
    lax.fori_loop(0, groups * n_frame, sent_over, 0)


def shards(
    n_tm,
    n_frame,
    start_state,
    initial_guess,
    noise_draws,
    timesteps,
    gain_space,
    gain_attention,
    time_weight,
    space_weight,
    attention_weight,
    output_weight,
):
    _, height, width, channels = start_state.shape
    cells = height * width
    part = cells // 2
    piece = part // n_frame
    groups = min(GROUPS, piece // 16)
    block = min(max(16, 128 // n_frame), piece // groups)
    half_width = channels // 2
    frequency = np.exp(-math.log(10000.0) * np.arange(half_width) / half_width).astype(np.float32)
    frequency = np.concatenate([frequency, frequency])[None]
    f32, bf16 = jnp.float32, jnp.bfloat16
    dma, vmem = pltpu.SemaphoreType.DMA, pltpu.VMEM
    field = vmem((cells, channels), f32)
    row = vmem((1, channels), f32)
    exchange = vmem((ITERS, groups, n_frame, 2 * piece // groups, channels), bf16)
    carried = vmem((ITERS, part + width, channels), bf16)
    anywhere = pl.BlockSpec(memory_space=pl.ANY)
    total = pl.pallas_call(
        functools.partial(kernel, n_tm, n_frame, width, groups),
        out_shape=pltpu.VMEM((cells, channels), f32),
        in_specs=[pl.BlockSpec(memory_space=pltpu.SMEM)] + [anywhere] * 10,
        out_specs=pl.BlockSpec(memory_space=pltpu.VMEM),
        scratch_shapes=[
            field,
            field,
            field,
            row,
            row,
            row,
            vmem(time_weight.shape, f32),
            vmem(space_weight.shape, bf16),
            vmem(attention_weight.shape, bf16),
            vmem(output_weight.shape, bf16),
            vmem((n_frame * block, n_frame * block), f32),
            vmem((2, 8, channels), f32),
            vmem((2, part, channels), bf16),
            vmem((2, part, channels), f32),
            vmem((cells + 2 * width, 3 * channels), bf16),
            vmem((2, part + 2 * width, 3 * channels), bf16),
            vmem((groups, n_frame, 2 * piece // groups, channels), f32),
            field,
            vmem((groups, n_frame, 2 * piece // groups, 3 * channels), bf16),
            exchange,
            exchange,
            exchange,
            exchange,
            vmem((cells, channels), bf16),
            vmem((part + width, channels), bf16),
            vmem((part + width, channels), f32),
            vmem((part, channels), bf16),
            vmem((2, n_frame, width, channels), bf16),
            vmem((2, width, channels), bf16),
            carried,
            carried,
            vmem((part, channels), bf16),
            vmem((part, channels), bf16),
            dma((11,)),
            *([dma((ITERS, groups, n_frame))] * 4),
            *([dma((groups, n_frame + 1))] * 2),
            *([dma((ITERS, groups, n_frame + 1))] * 2),
            *([dma((groups, n_frame))] * 2),
            *([dma((2,))] * 2),
            dma((2, n_frame)),
            dma((2,)),
            *([dma((groups, n_frame))] * 2),
        ],
        compiler_params=pltpu.CompilerParams(collective_id=0, has_side_effects=True),
    )(
        timesteps,
        start_state.reshape(cells, channels),
        initial_guess.reshape(cells, channels),
        noise_draws.reshape(cells, channels),
        jnp.asarray(frequency),
        gain_space[None],
        gain_attention[None],
        time_weight,
        space_weight,
        attention_weight,
        output_weight,
    )
    return total.reshape(1, 1, height, width, channels)


def solution(mesh):
    return jax.shard_map(
        functools.partial(shards, mesh.shape["tm"], mesh.shape["frame"]),
        mesh=mesh,
        in_specs=(
            P("frame", None, None, None),
            P("tm", "frame", None, None, None),
            P("tm", "frame", None, None, None),
            P("tm"),
            P(),
            P(),
            P(),
            P(),
            P(),
            P(),
        ),
        out_specs=P("tm", "frame", None, None, None),
        check_vma=False,
    )
```
